128 devices in a mesh: row: 8 (over x, y_lo), col: 16 (over z, y_hi, core).
Axes of the slice: x: 4, y: 4 (y_hi: 2, y_lo: 2; y = y_hi * 2 + y_lo), z: 4, core: 2. Of those that a mesh axis runs over, the one named last changes fastest.
Arguments:
- left_blocks: bfloat16 [8192, 8192], P('row', 'col'), may hold values from -6 to 6
- right_blocks: bfloat16 [8192, 8192], P('row', 'col'), may hold values from -0.09375 to 0.09375
- a_pattern: int32 [64, 64], P('row', 'col'), may hold values from 0 to 1, as said below
- b_pattern: int32 [64, 64], P('row', 'col'), may hold values 0 or 1
- keep_mask: int32 [64, 64], P('row', 'col'), may hold values 0 or 1
Outputs:
- product: bfloat16 [8192, 8192], P('row', 'col')
The draws below stay inside these ranges and needn't reach their ends.
Inputs may be any that keep to these rules, and one draw needn't show every extreme that they name: 1 marks a stored block; on average the share of stored blocks rises from about a quarter in the first block rows to about nine tenths in the last. A program may rely on no bound on the sum of `a_pattern` on one device or in one block row.
All inputs are finite; a program needn't handle non-finite values. No bound on the sum of `b_pattern` or of `keep_mask` on one device may be relied on, other than what follows from the above.
Results may differ from the reference program's by a relative error of at most 0.001.
Values may be sent and summed in bfloat16 or wider, within the bound.
A program may use at most 128 MiB of HBM per device.

```python
import jax
import jax.numpy as jnp

BLOCK = 128
A_BROWS = 64
K_BLOCKS = 64
N_BLOCKS = 64
M_ROWS = 8192
K_DIM = 8192
N_DIM = 8192


def draw_a_pattern(key, part):
    values = jax.random.randint(key, (A_BROWS, K_BLOCKS), 0, 100)
    levels = 25 + jnp.arange(A_BROWS, dtype=jnp.int32) * 65 // max(A_BROWS - 1, 1)
    return (values < levels[:, None]).astype(jnp.int32)


def with_ends(result, rng, smallest, top_value):
    place = [jax.random.randint(jax.random.fold_in(rng, axis), (), 0, length) for axis, length in enumerate(result.shape)]
    main_axis = result.shape.index(max(result.shape))
    neighbour = place[:main_axis] + [(place[main_axis] + 1) % result.shape[main_axis]] + place[main_axis + 1:]
    return result.at[tuple(place)].set(smallest).at[tuple(neighbour)].set(top_value)


def steps_of(own_key, dims, split, least, largest):
    factor_of = 1.0
    for position, shards_of in split:
        heights = jax.random.uniform(jax.random.fold_in(jax.random.fold_in(own_key, 6), position), (shards_of,), jnp.float32, least / len(split), largest / len(split))
        factor_of = factor_of * jnp.repeat(jnp.exp(heights), dims[position] // shards_of).reshape((-1,) + (1,) * (len(dims) - 1 - position))
    return factor_of


def gaussian(key, extent, width, reach, pieces=(), kind=jnp.bfloat16):
    gain = steps_of(key, extent, pieces, -0.22, 0.18) if pieces else 1.0
    values = jax.random.normal(key, extent, jnp.float32) * width * gain
    return jnp.minimum(jnp.maximum(values, -reach), reach).astype(kind)


def setup_inputs(seed: int = 0) -> dict:
    keys = jax.random.split(jax.random.key(seed), 6)
    return {
        "left_blocks": gaussian(keys[0], (M_ROWS, K_DIM), 1.0, 6.0, ((0, 8), (1, 16))),
        "right_blocks": gaussian(keys[1], (K_DIM, N_DIM), (K_DIM // 2) ** -0.5, 0.09375, ((0, 8), (1, 16))),
        "a_pattern": draw_a_pattern(jax.random.fold_in(keys[5], 71), 0),
        "b_pattern": with_ends((jax.random.randint(keys[3], (K_BLOCKS, N_BLOCKS), 0, 2) < 1).astype(jnp.int32), jax.random.fold_in(keys[3], 1), 0, 1),
        "keep_mask": with_ends((jax.random.randint(keys[4], (A_BROWS, N_BLOCKS), 0, 4) < 3).astype(jnp.int32), jax.random.fold_in(keys[4], 1), 0, 1),
    }


def expand_blocks(pattern_int, block_size):
    return jnp.repeat(jnp.repeat(pattern_int, block_size, axis=0), block_size, axis=1)


def reference(left_blocks, right_blocks, a_pattern, b_pattern, keep_mask):
    left_sparse = left_blocks * expand_blocks(a_pattern, BLOCK).astype(jnp.bfloat16)
    right_sparse = right_blocks * expand_blocks(b_pattern, BLOCK).astype(jnp.bfloat16)
    full_product = jnp.dot(left_sparse, right_sparse, preferred_element_type=jnp.float32)
    kept_cells = expand_blocks(keep_mask, BLOCK).astype(jnp.float32)
    return (full_product * kept_cells).astype(jnp.bfloat16)
```

```python
import jax
import jax.numpy as jnp
from jax import lax
from jax.experimental import pallas as pl
from jax.experimental.pallas import tpu as pltpu
from jax.sharding import PartitionSpec as P

MESH = pl.DeviceIdType.MESH
BLOCK = 128
ROWS = 1024
COLS = 512
PIECES = 4
PIECE = ROWS // PIECES
HALF = PIECES // 2

OWN, LEFT, RIGHT, FAR, P_OWN, P_LEFT, P_RIGHT, P_FAR = range(8)
RING_STEP = (0, 3, 1, 2, 0, 3, 1, 2)

FROM_LEFT = ((0, 160), (160, 160))
FROM_PLANE = ((320, 192), (512, 192))
FROM_RIGHT = ((704, 160), (864, 160))
FAR_PARTS = FROM_LEFT + FROM_PLANE + FROM_RIGHT
N_PARTS = 7 * PIECES + len(FAR_PARTS)


def pieces_of(origin):
    if origin == P_FAR:
        return FAR_PARTS
    return tuple((i * PIECE, PIECE) for i in range(PIECES))


def kernel(
    left_in, right_in, a_pat, b_pat, keep, out,
    a_all, b_all, total, load_sem, a_send, a_recv, b_send, b_recv, c_send, c_recv,
):
    row = lax.axis_index("row")
    col = lax.axis_index("col")
    x = row // 2
    y_lo = row % 2
    z = col // 4
    y_hi = col // 2 % 2
    core = col % 2

    x_up = ((x + 1) % 4 * 2 + y_lo, col)
    x_down = ((x + 3) % 4 * 2 + y_lo, col)
    b_plane = (x * 2 + 1 - y_lo, col)
    z_up = (row, (z + 1) % 4 * 4 + col % 4)
    z_down = (row, (z + 3) % 4 * 4 + col % 4)
    a_plane = (row, z * 4 + (1 - y_hi) * 2 + core)
    sibling = (row, col // 2 * 2 + 1 - core)

    def a_chunk(origin):
        plane = y_hi if origin < P_OWN else 1 - y_hi
        return (z + RING_STEP[origin]) % 4 * 2 + plane

    def b_chunk(origin):
        plane = y_lo if origin < P_OWN else 1 - y_lo
        return (x + RING_STEP[origin]) % 4 * 2 + plane

    barrier = pltpu.get_barrier_semaphore()
    partners = (x_up, x_down, b_plane, z_up, z_down, a_plane, sibling)
    for partner in partners:
        pl.semaphore_signal(barrier, inc=1, device_id=partner, device_id_type=MESH)

    a_own, b_own = a_chunk(OWN), b_chunk(OWN)
    loads = []
    for i in range(PIECES):
        rows = pl.ds(i * PIECE, PIECE)
        for which, (source, held) in enumerate(
            ((right_in, b_all.at[b_own]), (left_in, a_all.at[a_own, core]))
        ):
            load = pltpu.make_async_copy(
                source.at[rows], held.at[rows], load_sem.at[which, i]
            )
            load.start()
            loads.append(load)

    def mask(held, pattern, i):
        for bi in range(i * PIECE // BLOCK, (i + 1) * PIECE // BLOCK):
            for bj in range(COLS // BLOCK):
                cells = (pl.ds(bi * BLOCK, BLOCK), pl.ds(bj * BLOCK, BLOCK))
                stored = jnp.full((BLOCK, BLOCK), pattern[bi, bj].astype(jnp.float32))
                held[cells] = held[cells] * stored.astype(jnp.bfloat16)

    sent = []

    class Stream:
        def __init__(self, slot_of, send_sem, recv_sem):
            self.slot_of, self.send_sem, self.recv_sem = slot_of, send_sem, recv_sem
            self.count = 0

        def send(self, origin, span, to, arrives_as, index):
            ref = self.slot_of(origin).at[pl.ds(*span)]
            copy = pltpu.make_async_remote_copy(
                src_ref=ref,
                dst_ref=ref,
                send_sem=self.send_sem.at[self.count],
                recv_sem=self.recv_sem.at[arrives_as * PIECES + index],
                device_id=to,
                device_id_type=MESH,
            )
            self.count += 1
            copy.start()
            sent.append(copy)

        def wait(self, origin, index):
            ref = self.slot_of(origin).at[pl.ds(*pieces_of(origin)[index])]
            pltpu.make_async_remote_copy(
                src_ref=ref,
                dst_ref=ref,
                send_sem=self.send_sem.at[0],
                recv_sem=self.recv_sem.at[origin * PIECES + index],
                device_id=sibling,
                device_id_type=MESH,
            ).wait_recv()

    a_stream = Stream(lambda o: a_all.at[a_chunk(o), core], a_send, a_recv)
    b_stream = Stream(lambda o: b_all.at[b_chunk(o)], b_send, b_recv)
    c_stream = Stream(lambda o: a_all.at[a_chunk(o), core], c_send, c_recv)
    c_wait = Stream(lambda o: a_all.at[a_chunk(o), 1 - core], c_send, c_recv)

    def share(origin, index):
        c_stream.send(origin, pieces_of(origin)[index], sibling, origin, index)

    a_links = (a_stream, z_up, z_down, a_plane)
    b_links = (b_stream, x_up, x_down, b_plane)

    def arrived(links, origin, index):
        stream = links[0]
        stream.wait(origin, index)
        if stream is a_stream:
            share(origin, index)

    def send_own(links, i):
        stream, up, down, plane = links
        span = pieces_of(OWN)[i]
        stream.send(OWN, span, up, LEFT, i)
        stream.send(OWN, span, down, RIGHT, i)
        stream.send(OWN, span, plane, P_OWN, i)
        if stream is a_stream:
            share(OWN, i)

    for i in range(PIECES):
        loads[2 * i].wait()
        mask(b_all.at[b_own], b_pat, i)
        loads[2 * i + 1].wait()
        mask(a_all.at[a_own, core], a_pat, i)
        if i == 0:
            pl.semaphore_wait(barrier, len(partners))
        send_own(b_links, i)
        send_own(a_links, i)

    def ring_step(links, i):
        stream, up, down, _ = links
        arrived(links, LEFT, i)
        if i < HALF:
            stream.send(LEFT, pieces_of(LEFT)[i], up, FAR, i)
        arrived(links, RIGHT, i)
        if i >= HALF:
            stream.send(RIGHT, pieces_of(RIGHT)[i], down, FAR, i)

    def plane_step(links, i):
        stream, up, down, _ = links
        arrived(links, P_OWN, i)
        span = pieces_of(P_OWN)[i]
        stream.send(P_OWN, span, up, P_LEFT, i)
        stream.send(P_OWN, span, down, P_RIGHT, i)

    both = (b_links, a_links)
    for i in range(PIECES):
        for links in both:
            ring_step(links, i)
        if i % 2 == 1:
            for links in both:
                plane_step(links, i // 2)
    for i, j in ((0, HALF), (HALF - 1, PIECES - 1)):
        for links in both:
            for index in dict.fromkeys((i, j)):
                arrived(links, FAR, index)
    n_left, n_plane = len(FROM_LEFT), len(FROM_PLANE)
    for links in both:
        stream, plane = links[0], links[3]
        for k, span in enumerate(FROM_PLANE):
            stream.send(FAR, span, plane, P_FAR, n_left + k)
    for i in range(HALF, PIECES):
        for links in both:
            plane_step(links, i)
    for i in range(PIECES):
        for links in both:
            arrived(links, P_LEFT, i)
            if i == HALF - 1:
                for k, span in enumerate(FROM_LEFT):
                    links[0].send(P_LEFT, span, links[1], P_FAR, k)
            arrived(links, P_RIGHT, i)
            if i == PIECES - 1:
                for k, span in enumerate(FROM_RIGHT):
                    links[0].send(P_RIGHT, span, links[2], P_FAR, n_left + n_plane + k)
    for index in range(len(FAR_PARTS)):
        for links in both:
            arrived(links, P_FAR, index)
    for origin in range(8):
        for index in range(len(pieces_of(origin))):
            c_wait.wait(origin, index)

    for chunk in range(8):

        def multiply(i, _, chunk=chunk):
            rows = pl.ds(pl.multiple_of(i * 256, 256), 256)
            product = jnp.dot(
                a_all[chunk, 0, rows, :], b_all[chunk, 0:COLS, :],
                preferred_element_type=jnp.float32,
            ) + jnp.dot(
                a_all[chunk, 1, rows, :], b_all[chunk, COLS:ROWS, :],
                preferred_element_type=jnp.float32,
            )
            if chunk == 0:
                total[rows, :] = product
            else:
                total[rows, :] += product
            return 0

        lax.fori_loop(0, ROWS // 256, multiply, 0)

    def finish(i, _):
        rows = pl.ds(pl.multiple_of(i * BLOCK, BLOCK), BLOCK)
        for j in range(COLS // BLOCK):
            cols = pl.ds(j * BLOCK, BLOCK)
            kept = jnp.full((BLOCK, BLOCK), keep[i, j].astype(jnp.float32))
            out[rows, cols] = (total[rows, cols] * kept).astype(jnp.bfloat16)
        return 0

    lax.fori_loop(0, ROWS // BLOCK, finish, 0)
    for copy in sent:
        copy.wait_send()


def on_device(left_blocks, right_blocks, a_pattern, b_pattern, keep_mask):
    n_sends = 64
    return pl.pallas_call(
        kernel,
        out_shape=jax.ShapeDtypeStruct((ROWS, COLS), jnp.bfloat16),
        in_specs=[pl.BlockSpec(memory_space=pl.ANY)] * 2
        + [pl.BlockSpec(memory_space=pltpu.SMEM)] * 3,
        out_specs=pl.BlockSpec(memory_space=pltpu.VMEM),
        scratch_shapes=[
            pltpu.VMEM((8, 2, ROWS, COLS), jnp.bfloat16),
            pltpu.VMEM((8, ROWS, COLS), jnp.bfloat16),
            pltpu.VMEM((ROWS, COLS), jnp.float32),
            pltpu.SemaphoreType.DMA((2, PIECES)),
            pltpu.SemaphoreType.DMA((n_sends,)),
            pltpu.SemaphoreType.DMA((N_PARTS,)),
            pltpu.SemaphoreType.DMA((n_sends,)),
            pltpu.SemaphoreType.DMA((N_PARTS,)),
            pltpu.SemaphoreType.DMA((n_sends,)),
            pltpu.SemaphoreType.DMA((N_PARTS,)),
        ],
        compiler_params=pltpu.CompilerParams(
            collective_id=0,
            has_side_effects=True,
            vmem_limit_bytes=48 * 1024 * 1024,
        ),
    )(left_blocks, right_blocks, a_pattern, b_pattern, keep_mask)


def solution(mesh):
    placed = (P("row", "col"),) * 5
    return jax.shard_map(
        on_device, mesh=mesh, in_specs=placed, out_specs=P("row", "col"), check_vma=False
    )
```

```python
import jax
import jax.numpy as jnp
from jax import lax
from jax.experimental import pallas as pl
from jax.experimental.pallas import tpu as pltpu
from jax.sharding import PartitionSpec as P

MESH = pl.DeviceIdType.MESH
BLOCK = 128
ROWS = 1024
COLS = 512
PIECES = 4
PIECE = ROWS // PIECES
HALF = PIECES // 2

OWN, LEFT, RIGHT, FAR, P_OWN, P_LEFT, P_RIGHT, P_FAR = range(8)
RING_STEP = (0, 3, 1, 2, 0, 3, 1, 2)

A_FAR = ((0, 176), (176, 176), (352, 160), (512, 160), (672, 176), (848, 176))
B_FAR = ((0, 128), (128, 128), (256, 256), (512, 256), (768, 128), (896, 128))
PER_ORIGIN = 6


def kernel(
    left_in, right_in, a_pat_in, b_pat_in, keep_in, out,
    a_all, b_all, total, a_pat, b_pat, keep,
    load_sem, pat_sem, a_send, a_recv, b_send, b_recv, c_send, c_recv,
):
    row = lax.axis_index("row")
    col = lax.axis_index("col")
    x = row // 2
    y_lo = row % 2
    z = col // 4
    y_hi = col // 2 % 2
    core = col % 2

    x_up = ((x + 1) % 4 * 2 + y_lo, col)
    x_down = ((x + 3) % 4 * 2 + y_lo, col)
    b_plane = (x * 2 + 1 - y_lo, col)
    z_up = (row, (z + 1) % 4 * 4 + col % 4)
    z_down = (row, (z + 3) % 4 * 4 + col % 4)
    a_plane = (row, z * 4 + (1 - y_hi) * 2 + core)
    sibling = (row, col // 2 * 2 + 1 - core)

    def a_chunk(origin):
        plane = y_hi if origin < P_OWN else 1 - y_hi
        return (z + RING_STEP[origin]) % 4 * 2 + plane

    def b_chunk(origin):
        plane = y_lo if origin < P_OWN else 1 - y_lo
        return (x + RING_STEP[origin]) % 4 * 2 + plane

    barrier = pltpu.get_barrier_semaphore()
    partners = (x_up, x_down, b_plane, z_up, z_down, a_plane, sibling)
    for partner in partners:
        pl.semaphore_signal(barrier, inc=1, device_id=partner, device_id_type=MESH)

    a_own, b_own = a_chunk(OWN), b_chunk(OWN)
    patterns = [
        pltpu.make_async_copy(source, held, pat_sem.at[i])
        for i, (source, held) in enumerate(
            ((b_pat_in, b_pat), (a_pat_in, a_pat), (keep_in, keep))
        )
    ]
    for copy in patterns:
        copy.start()
    loads = []
    for i in range(PIECES):
        rows = pl.ds(i * PIECE, PIECE)
        for which, (source, held) in enumerate(
            ((right_in, b_all.at[b_own]), (left_in, a_all.at[a_own, core]))
        ):
            load = pltpu.make_async_copy(
                source.at[rows], held.at[rows], load_sem.at[which, i]
            )
            load.start()
            loads.append(load)

    def mask(held, pattern, i):
        for bi in range(i * PIECE // BLOCK, (i + 1) * PIECE // BLOCK):
            for bj in range(COLS // BLOCK):
                cells = (pl.ds(bi * BLOCK, BLOCK), pl.ds(bj * BLOCK, BLOCK))
                stored = jnp.full((BLOCK, BLOCK), pattern[bj, bi].astype(jnp.float32))
                held[cells] = held[cells] * stored.astype(jnp.bfloat16)

    sent = []

    class Stream:
        def __init__(self, slot_of, far, send_sem, recv_sem):
            self.slot_of, self.far = slot_of, far
            self.send_sem, self.recv_sem = send_sem, recv_sem
            self.count = 0

        def spans(self, origin):
            if origin == P_FAR:
                return self.far
            return tuple((i * PIECE, PIECE) for i in range(PIECES))

        def send(self, origin, span, to, arrives_as, index):
            ref = self.slot_of(origin).at[pl.ds(*span)]
            copy = pltpu.make_async_remote_copy(
                src_ref=ref,
                dst_ref=ref,
                send_sem=self.send_sem.at[self.count],
                recv_sem=self.recv_sem.at[arrives_as * PER_ORIGIN + index],
                device_id=to,
                device_id_type=MESH,
            )
            self.count += 1
            copy.start()
            sent.append(copy)

        def wait(self, origin, index):
            ref = self.slot_of(origin).at[pl.ds(*self.spans(origin)[index])]
            pltpu.make_async_remote_copy(
                src_ref=ref,
                dst_ref=ref,
                send_sem=self.send_sem.at[0],
                recv_sem=self.recv_sem.at[origin * PER_ORIGIN + index],
                device_id=sibling,
                device_id_type=MESH,
            ).wait_recv()

    a_stream = Stream(lambda o: a_all.at[a_chunk(o), core], A_FAR, a_send, a_recv)
    b_stream = Stream(lambda o: b_all.at[b_chunk(o)], B_FAR, b_send, b_recv)
    c_stream = Stream(lambda o: a_all.at[a_chunk(o), core], A_FAR, c_send, c_recv)
    c_wait = Stream(lambda o: a_all.at[a_chunk(o), 1 - core], A_FAR, c_send, c_recv)

    a_links = (a_stream, z_up, z_down, a_plane)
    b_links = (b_stream, x_up, x_down, b_plane)
    both = (b_links, a_links)

    def share(origin, index):
        c_stream.send(origin, a_stream.spans(origin)[index], sibling, origin, index)

    def arrived(links, origin, index):
        stream = links[0]
        stream.wait(origin, index)
        if stream is a_stream:
            share(origin, index)

    def shared(*origins):
        for origin in origins:
            for index in range(len(a_stream.spans(origin))):
                c_wait.wait(origin, index)

    def send_own(links, i):
        stream, up, down, plane = links
        span = stream.spans(OWN)[i]
        stream.send(OWN, span, up, LEFT, i)
        stream.send(OWN, span, down, RIGHT, i)
        stream.send(OWN, span, plane, P_OWN, i)
        if stream is a_stream:
            share(OWN, i)

    def ring_step(links, i):
        stream, up, down, _ = links
        arrived(links, LEFT, i)
        if i < HALF:
            stream.send(LEFT, stream.spans(LEFT)[i], up, FAR, i)
        arrived(links, RIGHT, i)
        if i >= HALF:
            stream.send(RIGHT, stream.spans(RIGHT)[i], down, FAR, i)

    def plane_step(links, i):
        stream, up, down, _ = links
        arrived(links, P_OWN, i)
        span = stream.spans(P_OWN)[i]
        stream.send(P_OWN, span, up, P_LEFT, i)
        stream.send(P_OWN, span, down, P_RIGHT, i)

    def partner_ring_step(links, i):
        stream, up, down, _ = links
        arrived(links, P_LEFT, i)
        if i == HALF - 1:
            for k in (0, 1):
                stream.send(P_LEFT, stream.far[k], up, P_FAR, k)
        arrived(links, P_RIGHT, i)
        if i == PIECES - 1:
            for k in (4, 5):
                stream.send(P_RIGHT, stream.far[k], down, P_FAR, k)

    def multiply(chunk, first=False):
        product = jnp.dot(
            a_all[chunk, 0], b_all[chunk, 0:COLS], preferred_element_type=jnp.float32
        ) + jnp.dot(
            a_all[chunk, 1], b_all[chunk, COLS:ROWS], preferred_element_type=jnp.float32
        )
        if first:
            total[...] = product
        else:
            total[...] += product

    meet = 1 - (y_hi + y_lo) % 2
    turn = (x + 4 - z) % 4
    odd = turn % 2

    def choose(if_meet, otherwise):
        return meet * if_meet + (1 - meet) * otherwise

    def partner_chunk(step):
        return (z + step) % 4 * 2 + 1 - y_hi

    early = (
        choose(a_chunk(OWN), b_chunk(P_OWN)),
        choose(a_chunk(FAR), a_chunk(P_OWN)),
    )
    middle = (
        choose(a_chunk(LEFT), b_chunk(P_LEFT)),
        choose(a_chunk(RIGHT), b_chunk(P_RIGHT)),
        choose(partner_chunk(1 - odd), a_chunk(P_LEFT)),
        choose(partner_chunk((1 - odd) * 3 + odd * turn), a_chunk(P_RIGHT)),
    )
    b_late = choose(partner_chunk(odd * (4 - turn)), b_chunk(P_FAR))
    a_late = a_chunk(P_FAR)

    for copy in patterns[:2]:
        copy.wait()
    for i in range(PIECES):
        loads[2 * i].wait()
        mask(b_all.at[b_own], b_pat, i)
        loads[2 * i + 1].wait()
        mask(a_all.at[a_own, core], a_pat, i)
        if i == 0:
            pl.semaphore_wait(barrier, len(partners))
        send_own(b_links, i)
        send_own(a_links, i)

    for i in range(PIECES):
        for links in both:
            ring_step(links, i)
        if i % 2 == 1:
            for links in both:
                plane_step(links, i // 2)
    for i, j in ((0, HALF), (HALF - 1, PIECES - 1)):
        for links in both:
            for index in dict.fromkeys((i, j)):
                arrived(links, FAR, index)
    for links in both:
        stream, plane = links[0], links[3]
        for k in (2, 3):
            stream.send(FAR, stream.far[k], plane, P_FAR, k)
    for i in range(HALF, PIECES):
        for links in both:
            plane_step(links, i)
    shared(OWN, LEFT, RIGHT, FAR, P_OWN)
    multiply(early[0], first=True)
    for links in both:
        partner_ring_step(links, 0)
    multiply(early[1])
    for i in range(1, PIECES):
        for links in both:
            partner_ring_step(links, i)
    shared(P_LEFT, P_RIGHT)
    for n, chunk in enumerate(middle):
        multiply(chunk)
        if n >= 2:
            arrived(a_links, P_FAR, n)
    for k in (2, 3, 0, 4, 1, 5):
        arrived(b_links, P_FAR, k)
        if k in (0, 4):
            arrived(a_links, P_FAR, k)
        first, rows = B_FAR[k]
        total[...] += jnp.dot(
            a_all[b_late, first // COLS, :, first % COLS : first % COLS + rows],
            b_all[b_late, first : first + rows],
            preferred_element_type=jnp.float32,
        )
    for k in (1, 5):
        arrived(a_links, P_FAR, k)
    for k in (2, 3, 0, 4, 1, 5):
        first, rows = A_FAR[k]
        cells = pl.ds(first, rows)
        c_wait.wait(P_FAR, k)
        total[cells] += jnp.dot(
            a_all[a_late, 0, cells], b_all[a_late, 0:COLS],
            preferred_element_type=jnp.float32,
        ) + jnp.dot(
            a_all[a_late, 1, cells], b_all[a_late, COLS:ROWS],
            preferred_element_type=jnp.float32,
        )

    patterns[2].wait()

    def finish(i, _):
        rows = pl.ds(pl.multiple_of(i * BLOCK, BLOCK), BLOCK)
        for j in range(COLS // BLOCK):
            cols = pl.ds(j * BLOCK, BLOCK)
            kept = jnp.full((BLOCK, BLOCK), keep[j, i].astype(jnp.float32))
            out[rows, cols] = (total[rows, cols] * kept).astype(jnp.bfloat16)
        return 0

    lax.fori_loop(0, ROWS // BLOCK, finish, 0)
    for copy in sent:
        copy.wait_send()


def on_device(left_blocks, right_blocks, a_pattern, b_pattern, keep_mask):
    n_sends = 64
    n_parts = 8 * PER_ORIGIN
    pattern = pltpu.SMEM(keep_mask.T.shape, jnp.int32)
    return pl.pallas_call(
        kernel,
        out_shape=jax.ShapeDtypeStruct((ROWS, COLS), jnp.bfloat16),
        in_specs=[pl.BlockSpec(memory_space=pltpu.HBM)] * 5,
        out_specs=pl.BlockSpec(memory_space=pltpu.VMEM),
        scratch_shapes=[
            pltpu.VMEM((8, 2, ROWS, COLS), jnp.bfloat16),
            pltpu.VMEM((8, ROWS, COLS), jnp.bfloat16),
            pltpu.VMEM((ROWS, COLS), jnp.float32),
            pattern,
            pattern,
            pattern,
            pltpu.SemaphoreType.DMA((2, PIECES)),
            pltpu.SemaphoreType.DMA((3,)),
            pltpu.SemaphoreType.DMA((n_sends,)),
            pltpu.SemaphoreType.DMA((n_parts,)),
            pltpu.SemaphoreType.DMA((n_sends,)),
            pltpu.SemaphoreType.DMA((n_parts,)),
            pltpu.SemaphoreType.DMA((n_sends,)),
            pltpu.SemaphoreType.DMA((n_parts,)),
        ],
        compiler_params=pltpu.CompilerParams(
            collective_id=0,
            has_side_effects=True,
            vmem_limit_bytes=40 * 1024 * 1024,
        ),
    )(*[pltpu.with_memory_space_constraint(v, pltpu.HBM) for v in (left_blocks, right_blocks, a_pattern.T, b_pattern.T, keep_mask.T)])


def solution(mesh):
    placed = (P("row", "col"),) * 5
    return jax.shard_map(
        on_device, mesh=mesh, in_specs=placed, out_specs=P("row", "col"), check_vma=False
    )
```

```python
import jax
import jax.numpy as jnp
from jax import lax
from jax.experimental import pallas as pl
from jax.experimental.pallas import tpu as pltpu
from jax.sharding import PartitionSpec as P

MESH = pl.DeviceIdType.MESH
BLOCK = 128
ROWS = 1024
COLS = 512
PIECES = 4
PIECE = ROWS // PIECES
HALF = PIECES // 2

OWN, LEFT, RIGHT, FAR, P_OWN, P_LEFT, P_RIGHT, P_FAR = range(8)
RING_STEP = (0, 3, 1, 2, 0, 3, 1, 2)

A_FAR = (
    ((0, 128), (128, 128)),
    ((256, 128), (384, 128)),
    ((512, 256), (768, 256)),
)
B_FAR = (
    ((256, 96), (0, 128), (128, 128)),
    ((352, 160), (512, 128), (640, 64)),
    ((704, 64), (768, 256)),
)
PER_ORIGIN = 8


def kernel(
    left_in, right_in, a_pat_in, b_pat_in, keep_in, out,
    a_all, b_all, total, a_pat, b_pat, keep,
    load_sem, pat_sem, a_send, a_recv, b_send, b_recv, c_send, c_recv,
):
    row = lax.axis_index("row")
    col = lax.axis_index("col")
    x = row // 2
    y_lo = row % 2
    z = col // 4
    y_hi = col // 2 % 2
    core = col % 2

    x_up = ((x + 1) % 4 * 2 + y_lo, col)
    x_down = ((x + 3) % 4 * 2 + y_lo, col)
    b_plane = (x * 2 + 1 - y_lo, col)
    z_up = (row, (z + 1) % 4 * 4 + col % 4)
    z_down = (row, (z + 3) % 4 * 4 + col % 4)
    a_plane = (row, z * 4 + (1 - y_hi) * 2 + core)
    sibling = (row, col // 2 * 2 + 1 - core)

    def a_chunk(origin):
        plane = y_hi if origin < P_OWN else 1 - y_hi
        return (z + RING_STEP[origin]) % 4 * 2 + plane

    def b_chunk(origin):
        plane = y_lo if origin < P_OWN else 1 - y_lo
        return (x + RING_STEP[origin]) % 4 * 2 + plane

    barrier = pltpu.get_barrier_semaphore()
    partners = (x_up, x_down, b_plane, z_up, z_down, a_plane, sibling)
    for partner in partners:
        pl.semaphore_signal(barrier, inc=1, device_id=partner, device_id_type=MESH)

    a_own, b_own = a_chunk(OWN), b_chunk(OWN)
    patterns = [
        pltpu.make_async_copy(source, held, pat_sem.at[i])
        for i, (source, held) in enumerate(
            ((b_pat_in, b_pat), (a_pat_in, a_pat), (keep_in, keep))
        )
    ]
    for copy in patterns:
        copy.start()
    loads = []
    for i in range(PIECES):
        rows = pl.ds(i * PIECE, PIECE)
        for which, (source, held) in enumerate(
            ((right_in, b_all.at[b_own]), (left_in, a_all.at[a_own, core]))
        ):
            load = pltpu.make_async_copy(
                source.at[rows], held.at[rows], load_sem.at[which, i]
            )
            load.start()
            loads.append(load)

    def mask(held, pattern, i):
        for bi in range(i * PIECE // BLOCK, (i + 1) * PIECE // BLOCK):
            for bj in range(COLS // BLOCK):
                cells = (pl.ds(bi * BLOCK, BLOCK), pl.ds(bj * BLOCK, BLOCK))
                stored = jnp.full((BLOCK, BLOCK), pattern[bj, bi].astype(jnp.float32))
                held[cells] = held[cells] * stored.astype(jnp.bfloat16)

    sent = []

    class Stream:
        def __init__(self, slot_of, far, send_sem, recv_sem):
            self.slot_of, self.far = slot_of, far[0] + far[1] + far[2]
            self.n_up, self.n_down = len(far[0]), len(far[1])
            self.forwarded = 0
            self.send_sem, self.recv_sem = send_sem, recv_sem
            self.count = 0

        def spans(self, origin):
            if origin == P_FAR:
                return self.far
            return tuple((i * PIECE, PIECE) for i in range(PIECES))

        def send(self, origin, span, to, arrives_as, index):
            ref = self.slot_of(origin).at[pl.ds(*span)]
            copy = pltpu.make_async_remote_copy(
                src_ref=ref,
                dst_ref=ref,
                send_sem=self.send_sem.at[self.count],
                recv_sem=self.recv_sem.at[arrives_as * PER_ORIGIN + index],
                device_id=to,
                device_id_type=MESH,
            )
            self.count += 1
            copy.start()
            sent.append(copy)

        def wait(self, origin, index):
            ref = self.slot_of(origin).at[pl.ds(*self.spans(origin)[index])]
            pltpu.make_async_remote_copy(
                src_ref=ref,
                dst_ref=ref,
                send_sem=self.send_sem.at[0],
                recv_sem=self.recv_sem.at[origin * PER_ORIGIN + index],
                device_id=sibling,
                device_id_type=MESH,
            ).wait_recv()

    a_stream = Stream(lambda o: a_all.at[a_chunk(o), core], A_FAR, a_send, a_recv)
    b_stream = Stream(lambda o: b_all.at[b_chunk(o)], B_FAR, b_send, b_recv)
    c_stream = Stream(lambda o: a_all.at[a_chunk(o), core], A_FAR, c_send, c_recv)
    c_wait = Stream(lambda o: a_all.at[a_chunk(o), 1 - core], A_FAR, c_send, c_recv)

    a_links = (a_stream, z_up, z_down, a_plane)
    b_links = (b_stream, x_up, x_down, b_plane)
    both = (b_links, a_links)

    def share(origin, index):
        c_stream.send(origin, a_stream.spans(origin)[index], sibling, origin, index)

    def arrived(links, origin, index):
        stream = links[0]
        stream.wait(origin, index)
        if stream is a_stream:
            share(origin, index)

    def shared(*origins):
        for origin in origins:
            for index in range(len(a_stream.spans(origin))):
                c_wait.wait(origin, index)

    def send_own(links, i):
        stream, up, down, plane = links
        span = stream.spans(OWN)[i]
        stream.send(OWN, span, up, LEFT, i)
        stream.send(OWN, span, down, RIGHT, i)
        stream.send(OWN, span, plane, P_OWN, i)
        if stream is a_stream:
            share(OWN, i)

    def ring_step(links, i):
        stream, up, down, _ = links
        arrived(links, LEFT, i)
        if i < HALF:
            stream.send(LEFT, stream.spans(LEFT)[i], up, FAR, i)
        arrived(links, RIGHT, i)
        if i >= HALF:
            stream.send(RIGHT, stream.spans(RIGHT)[i], down, FAR, i)

    def plane_step(links, i):
        stream, up, down, _ = links
        arrived(links, P_OWN, i)
        span = stream.spans(P_OWN)[i]
        stream.send(P_OWN, span, up, P_LEFT, i)
        stream.send(P_OWN, span, down, P_RIGHT, i)

    def forward(links, origin, to, first, stop, i):
        stream = links[0]
        covered = [span[0] + span[1] <= (i + 1) * PIECE for span in stream.far[first:stop]]
        before = [span[0] + span[1] <= i * PIECE for span in stream.far[first:stop]]
        if all(covered) and not all(before):
            for k in range(first, stop):
                stream.send(origin, stream.far[k], to, P_FAR, k)

    def partner_ring_step(links, i):
        stream, up, down, _ = links
        n_up, n_down = stream.n_up, stream.n_down
        arrived(links, P_LEFT, i)
        forward(links, P_LEFT, up, 0, n_up, i)
        arrived(links, P_RIGHT, i)
        forward(links, P_RIGHT, down, n_up, n_up + n_down, i)

    def plane_far(links):
        stream, plane = links[0], links[3]
        for k in range(stream.n_up + stream.n_down, len(stream.far)):
            stream.send(FAR, stream.far[k], plane, P_FAR, k)

    def multiply(chunk, first=False):
        product = jnp.dot(
            a_all[chunk, 0], b_all[chunk, 0:COLS], preferred_element_type=jnp.float32
        ) + jnp.dot(
            a_all[chunk, 1], b_all[chunk, COLS:ROWS], preferred_element_type=jnp.float32
        )
        if first:
            total[...] = product
        else:
            total[...] += product

    def add_depth(chunk, first, rows):
        total[...] += jnp.dot(
            a_all[chunk, first // COLS, :, first % COLS : first % COLS + rows],
            b_all[chunk, first : first + rows],
            preferred_element_type=jnp.float32,
        )

    def add_rows(chunk, first, rows):
        cells = pl.ds(first, rows)
        total[cells] += jnp.dot(
            a_all[chunk, 0, cells], b_all[chunk, 0:COLS],
            preferred_element_type=jnp.float32,
        ) + jnp.dot(
            a_all[chunk, 1, cells], b_all[chunk, COLS:ROWS],
            preferred_element_type=jnp.float32,
        )

    meet = 1 - (y_hi + y_lo) % 2
    turn = (x + 4 - z) % 4
    odd = turn % 2
    turned = (turn + 3) // 4

    def choose(if_meet, otherwise):
        return meet * if_meet + (1 - meet) * otherwise

    def partner_chunk(step):
        return (z + step) % 4 * 2 + 1 - y_hi

    early = (
        choose(a_chunk(OWN), b_chunk(P_OWN)),
        choose(a_chunk(FAR), a_chunk(P_OWN)),
    )
    middle = (
        choose(a_chunk(LEFT), b_chunk(P_LEFT)),
        choose(a_chunk(RIGHT), b_chunk(P_RIGHT)),
        choose(partner_chunk(1 - odd), a_chunk(P_LEFT)),
        choose(partner_chunk((1 - odd) * 3 + odd * turn), a_chunk(P_RIGHT)),
    )
    a_late = choose(partner_chunk(2 * turned), a_chunk(P_FAR))
    b_late = b_chunk(P_FAR)

    for copy in patterns[:2]:
        copy.wait()
    for i in range(PIECES):
        loads[2 * i].wait()
        mask(b_all.at[b_own], b_pat, i)
        if i == 0:
            pl.semaphore_wait(barrier, len(partners))
        send_own(b_links, i)
        loads[2 * i + 1].wait()
        mask(a_all.at[a_own, core], a_pat, i)
        send_own(a_links, i)

    for i in range(PIECES):
        for links in both:
            ring_step(links, i)
    for i in range(PIECES - 1):
        for links in both:
            plane_step(links, i)
    for i, j in ((0, HALF), (HALF - 1, PIECES - 1)):
        for links in both:
            for index in dict.fromkeys((i, j)):
                arrived(links, FAR, index)
    for links in both[::-1]:
        plane_far(links)
    for links in both:
        plane_step(links, PIECES - 1)
    shared(OWN, LEFT, RIGHT, FAR, P_OWN)
    multiply(early[0], first=True)
    for links in both:
        partner_ring_step(links, 0)
    multiply(early[1])
    for links in both:
        partner_ring_step(links, 1)
    add_depth(middle[0], 0, COLS)
    add_depth(middle[1], 0, COLS)
    for i in range(HALF, PIECES):
        for links in both:
            partner_ring_step(links, i)
    shared(P_LEFT, P_RIGHT)
    add_depth(middle[0], COLS, COLS)
    add_depth(middle[1], COLS, COLS)
    multiply(middle[2])
    for k in (4, 5):
        arrived(a_links, P_FAR, k)
    for k in (0, 2):
        arrived(a_links, P_FAR, k)
    multiply(middle[3])
    for k in (1, 3):
        arrived(a_links, P_FAR, k)
    for k in (4, 5):
        c_wait.wait(P_FAR, k)
    add_rows(a_late, 512, 512)
    for k in range(4):
        c_wait.wait(P_FAR, k)
    add_rows(a_late, 0, 512)
    for k in (0, 3, 1, 2):
        arrived(b_links, P_FAR, k)
    add_depth(b_late, 0, 512)
    for k in (4, 5, 6, 7):
        arrived(b_links, P_FAR, k)
    add_depth(b_late, 512, 512)

    patterns[2].wait()

    def finish(i, _):
        rows = pl.ds(pl.multiple_of(i * BLOCK, BLOCK), BLOCK)
        for j in range(COLS // BLOCK):
            cols = pl.ds(j * BLOCK, BLOCK)
            kept = jnp.full((BLOCK, BLOCK), keep[j, i].astype(jnp.float32))
            out[rows, cols] = (total[rows, cols] * kept).astype(jnp.bfloat16)
        return 0

    lax.fori_loop(0, ROWS // BLOCK, finish, 0)
    for copy in sent:
        copy.wait_send()


def on_device(left_blocks, right_blocks, a_pattern, b_pattern, keep_mask):
    n_sends = 64
    n_parts = 8 * PER_ORIGIN
    pattern = pltpu.SMEM(keep_mask.T.shape, jnp.int32)
    return pl.pallas_call(
        kernel,
        out_shape=jax.ShapeDtypeStruct((ROWS, COLS), jnp.bfloat16),
        in_specs=[pl.BlockSpec(memory_space=pltpu.HBM)] * 5,
        out_specs=pl.BlockSpec(memory_space=pltpu.VMEM),
        scratch_shapes=[
            pltpu.VMEM((8, 2, ROWS, COLS), jnp.bfloat16),
            pltpu.VMEM((8, ROWS, COLS), jnp.bfloat16),
            pltpu.VMEM((ROWS, COLS), jnp.float32),
            pattern,
            pattern,
            pattern,
            pltpu.SemaphoreType.DMA((2, PIECES)),
            pltpu.SemaphoreType.DMA((3,)),
            pltpu.SemaphoreType.DMA((n_sends,)),
            pltpu.SemaphoreType.DMA((n_parts,)),
            pltpu.SemaphoreType.DMA((n_sends,)),
            pltpu.SemaphoreType.DMA((n_parts,)),
            pltpu.SemaphoreType.DMA((n_sends,)),
            pltpu.SemaphoreType.DMA((n_parts,)),
        ],
        compiler_params=pltpu.CompilerParams(
            collective_id=0,
            has_side_effects=True,
            vmem_limit_bytes=40 * 1024 * 1024,
        ),
    )(*[pltpu.with_memory_space_constraint(v, pltpu.HBM) for v in (left_blocks, right_blocks, a_pattern.T, b_pattern.T, keep_mask.T)])


def solution(mesh):
    placed = (P("row", "col"),) * 5
    return jax.shard_map(
        on_device, mesh=mesh, in_specs=placed, out_specs=P("row", "col"), check_vma=False
    )
```

```python
import jax
import jax.numpy as jnp
from jax import lax
from jax.experimental import pallas as pl
from jax.experimental.pallas import tpu as pltpu
from jax.sharding import PartitionSpec as P

MESH = pl.DeviceIdType.MESH
BLOCK = 128
ROWS = 1024
COLS = 512
PIECES = 4
PIECE = ROWS // PIECES
HALF = PIECES // 2

OWN, LEFT, RIGHT, FAR, P_OWN, P_LEFT, P_RIGHT, P_FAR = range(8)
RING_STEP = (0, 3, 1, 2, 0, 3, 1, 2)

A_FAR = (
    ((0, 112), (112, 128)),
    ((368, 112), (240, 128)),
    ((480, 272), (752, 272)),
)
B_FAR = (
    ((128, 224), (0, 128)),
    ((352, 160), (512, 128), (640, 64)),
    ((768, 256), (704, 64)),
)
PER_ORIGIN = 8
ALL = (0, ROWS)


def kernel(
    left_in, right_in, a_pat_in, b_pat_in, keep_in, out,
    a_all, b_all, total, a_pat, b_pat, keep,
    load_sem, pat_sem, a_send, a_recv, b_send, b_recv, c_send, c_recv,
):
    row = lax.axis_index("row")
    col = lax.axis_index("col")
    x = row // 2
    y_lo = row % 2
    z = col // 4
    y_hi = col // 2 % 2
    core = col % 2

    x_up = ((x + 1) % 4 * 2 + y_lo, col)
    x_down = ((x + 3) % 4 * 2 + y_lo, col)
    b_plane = (x * 2 + 1 - y_lo, col)
    z_up = (row, (z + 1) % 4 * 4 + col % 4)
    z_down = (row, (z + 3) % 4 * 4 + col % 4)
    a_plane = (row, z * 4 + (1 - y_hi) * 2 + core)
    sibling = (row, col // 2 * 2 + 1 - core)

    def a_chunk(origin):
        plane = y_hi if origin < P_OWN else 1 - y_hi
        return (z + RING_STEP[origin]) % 4 * 2 + plane

    def b_chunk(origin):
        plane = y_lo if origin < P_OWN else 1 - y_lo
        return (x + RING_STEP[origin]) % 4 * 2 + plane

    barrier = pltpu.get_barrier_semaphore()
    partners = (x_up, x_down, b_plane, z_up, z_down, a_plane, sibling)
    for partner in partners:
        pl.semaphore_signal(barrier, inc=1, device_id=partner, device_id_type=MESH)

    a_own, b_own = a_chunk(OWN), b_chunk(OWN)
    patterns = [
        pltpu.make_async_copy(source, held, pat_sem.at[i])
        for i, (source, held) in enumerate(
            ((b_pat_in, b_pat), (a_pat_in, a_pat), (keep_in, keep))
        )
    ]
    for copy in patterns:
        copy.start()
    loads = []
    for i in range(PIECES):
        rows = pl.ds(i * PIECE, PIECE)
        for which, (source, held) in enumerate(
            ((right_in, b_all.at[b_own]), (left_in, a_all.at[a_own, core]))
        ):
            load = pltpu.make_async_copy(
                source.at[rows], held.at[rows], load_sem.at[which, i]
            )
            load.start()
            loads.append(load)

    def mask(held, pattern, i):
        for bi in range(i * PIECE // BLOCK, (i + 1) * PIECE // BLOCK):
            for bj in range(COLS // BLOCK):
                cells = (pl.ds(bi * BLOCK, BLOCK), pl.ds(bj * BLOCK, BLOCK))
                stored = jnp.full((BLOCK, BLOCK), pattern[bj, bi].astype(jnp.float32))
                held[cells] = held[cells] * stored.astype(jnp.bfloat16)

    sent = []

    class Stream:
        def __init__(self, slot_of, far, send_sem, recv_sem):
            self.slot_of, self.far = slot_of, far[0] + far[1] + far[2]
            self.n_up, self.n_down = len(far[0]), len(far[1])
            self.forwarded = 0
            self.send_sem, self.recv_sem = send_sem, recv_sem
            self.count = 0

        def spans(self, origin):
            if origin == P_FAR:
                return self.far
            return tuple((i * PIECE, PIECE) for i in range(PIECES))

        def send(self, origin, span, to, arrives_as, index):
            ref = self.slot_of(origin).at[pl.ds(*span)]
            copy = pltpu.make_async_remote_copy(
                src_ref=ref,
                dst_ref=ref,
                send_sem=self.send_sem.at[self.count],
                recv_sem=self.recv_sem.at[arrives_as * PER_ORIGIN + index],
                device_id=to,
                device_id_type=MESH,
            )
            self.count += 1
            copy.start()
            sent.append(copy)

        def wait(self, origin, index):
            ref = self.slot_of(origin).at[pl.ds(*self.spans(origin)[index])]
            pltpu.make_async_remote_copy(
                src_ref=ref,
                dst_ref=ref,
                send_sem=self.send_sem.at[0],
                recv_sem=self.recv_sem.at[origin * PER_ORIGIN + index],
                device_id=sibling,
                device_id_type=MESH,
            ).wait_recv()

    a_stream = Stream(lambda o: a_all.at[a_chunk(o), core], A_FAR, a_send, a_recv)
    b_stream = Stream(lambda o: b_all.at[b_chunk(o)], B_FAR, b_send, b_recv)
    c_stream = Stream(lambda o: a_all.at[a_chunk(o), core], A_FAR, c_send, c_recv)
    c_wait = Stream(lambda o: a_all.at[a_chunk(o), 1 - core], A_FAR, c_send, c_recv)

    a_links = (a_stream, z_up, z_down, a_plane)
    b_links = (b_stream, x_up, x_down, b_plane)
    both = (b_links, a_links)

    def share(origin, index):
        c_stream.send(origin, a_stream.spans(origin)[index], sibling, origin, index)

    def arrived(links, origin, index):
        stream = links[0]
        stream.wait(origin, index)
        if stream is a_stream:
            share(origin, index)

    def shared(*origins):
        for origin in origins:
            for index in range(len(a_stream.spans(origin))):
                c_wait.wait(origin, index)

    def shared_span(origin, *indices):
        for index in indices:
            c_wait.wait(origin, index)

    def send_own(links, i):
        stream, up, down, plane = links
        span = stream.spans(OWN)[i]
        stream.send(OWN, span, up, LEFT, i)
        stream.send(OWN, span, down, RIGHT, i)
        stream.send(OWN, span, plane, P_OWN, i)
        if stream is a_stream:
            share(OWN, i)

    def ring_step(links, i):
        stream, up, down, _ = links
        arrived(links, LEFT, i)
        if i < HALF:
            stream.send(LEFT, stream.spans(LEFT)[i], up, FAR, i)
        arrived(links, RIGHT, i)
        if i >= HALF:
            stream.send(RIGHT, stream.spans(RIGHT)[i], down, FAR, i)

    def plane_step(links, i):
        stream, up, down, _ = links
        arrived(links, P_OWN, i)
        span = stream.spans(P_OWN)[i]
        stream.send(P_OWN, span, up, P_LEFT, i)
        stream.send(P_OWN, span, down, P_RIGHT, i)

    def forward(links, origin, to, first, stop, i):
        stream = links[0]
        covered = [span[0] + span[1] <= (i + 1) * PIECE for span in stream.far[first:stop]]
        before = [span[0] + span[1] <= i * PIECE for span in stream.far[first:stop]]
        if all(covered) and not all(before):
            for k in range(first, stop):
                stream.send(origin, stream.far[k], to, P_FAR, k)

    def partner_ring_step(links, i):
        stream, up, down, _ = links
        n_up, n_down = stream.n_up, stream.n_down
        arrived(links, P_LEFT, i)
        forward(links, P_LEFT, up, 0, n_up, i)
        arrived(links, P_RIGHT, i)
        forward(links, P_RIGHT, down, n_up, n_up + n_down, i)

    def plane_far(links):
        stream, plane = links[0], links[3]
        for k in range(stream.n_up + stream.n_down, len(stream.far)):
            stream.send(FAR, stream.far[k], plane, P_FAR, k)

    def part_of(chunk, rows, depth):
        cells = pl.ds(*rows)
        first, count = depth
        half, start = first // COLS, first % COLS
        return jnp.dot(
            a_all[chunk, half, cells, start : start + count],
            b_all[chunk, first : first + count],
            preferred_element_type=jnp.float32,
        )

    def add(chunk, rows, depth):
        total[pl.ds(*rows)] += part_of(chunk, rows, depth)

    def product_of(chunk, rows):
        cells = pl.ds(*rows)
        return jnp.dot(
            a_all[chunk, 0, cells], b_all[chunk, 0:COLS],
            preferred_element_type=jnp.float32,
        ) + jnp.dot(
            a_all[chunk, 1, cells], b_all[chunk, COLS:ROWS],
            preferred_element_type=jnp.float32,
        )

    def finish(rows, added):
        first, count = rows
        result = total[pl.ds(*rows)] + added
        for bi in range(count // BLOCK):
            for bj in range(COLS // BLOCK):
                kept = keep[bj, first // BLOCK + bi].astype(jnp.float32)
                block = result[
                    bi * BLOCK : (bi + 1) * BLOCK, bj * BLOCK : (bj + 1) * BLOCK
                ]
                out[
                    pl.ds(first + bi * BLOCK, BLOCK), pl.ds(bj * BLOCK, BLOCK)
                ] = (block * kept).astype(jnp.bfloat16)

    meet = 1 - (y_hi + y_lo) % 2
    turn = (x + 4 - z) % 4
    odd = turn % 2
    turned = (turn + 3) // 4

    def choose(if_meet, otherwise):
        return meet * if_meet + (1 - meet) * otherwise

    def partner_chunk(step):
        return (z + step) % 4 * 2 + 1 - y_hi

    early = (
        choose(a_chunk(OWN), b_chunk(P_OWN)),
        choose(a_chunk(FAR), a_chunk(P_OWN)),
    )
    middle = (
        choose(a_chunk(LEFT), b_chunk(P_LEFT)),
        choose(a_chunk(RIGHT), b_chunk(P_RIGHT)),
        choose(partner_chunk(1 - odd), a_chunk(P_LEFT)),
        choose(partner_chunk((1 - odd) * 3 + odd * turn), a_chunk(P_RIGHT)),
    )
    a_late = choose(partner_chunk(2 * turned), a_chunk(P_FAR))
    b_late = b_chunk(P_FAR)

    for copy in patterns[:2]:
        copy.wait()
    for i in range(PIECES):
        loads[2 * i].wait()
        mask(b_all.at[b_own], b_pat, i)
        if i == 0:
            pl.semaphore_wait(barrier, len(partners))
        send_own(b_links, i)
        loads[2 * i + 1].wait()
        mask(a_all.at[a_own, core], a_pat, i)
        send_own(a_links, i)

    for i in range(PIECES):
        for links in both:
            ring_step(links, i)
    for i in range(PIECES - 1):
        for links in both:
            plane_step(links, i)
    for i, j in ((0, HALF), (HALF - 1, PIECES - 1)):
        for links in both:
            for index in dict.fromkeys((i, j)):
                arrived(links, FAR, index)
    for links in both[::-1]:
        plane_far(links)
    for links in both:
        plane_step(links, PIECES - 1)
    shared(OWN, LEFT, RIGHT, FAR, P_OWN)
    total[...] = product_of(early[0], ALL)
    for links in both:
        partner_ring_step(links, 0)
    total[...] += product_of(early[1], ALL)
    for links in both:
        partner_ring_step(links, 1)
    add(middle[0], ALL, (0, 512))
    add(middle[1], ALL, (0, 512))
    shared_span(P_LEFT, 0, 1)
    shared_span(P_RIGHT, 0, 1)
    add(middle[2], (0, 512), (0, 512))
    add(middle[3], (0, 512), (0, 512))
    for links in both:
        partner_ring_step(links, 2)
    add(middle[0], ALL, (512, 256))
    add(middle[1], ALL, (512, 256))
    for links in both:
        partner_ring_step(links, 3)
    add(middle[0], ALL, (768, 256))
    add(middle[1], ALL, (768, 256))
    shared_span(P_LEFT, 2, 3)
    shared_span(P_RIGHT, 2, 3)
    add(middle[2], (512, 512), (0, 512))
    add(middle[3], (512, 512), (0, 512))
    ringed = list(sent)
    for k in (4, 5):
        arrived(a_links, P_FAR, k)
    add(middle[2], ALL, (512, 512))
    for k in (0, 2):
        arrived(a_links, P_FAR, k)
    add(middle[3], ALL, (512, 512))
    for copy in ringed:
        copy.wait_send()
    for k in (1, 3):
        arrived(a_links, P_FAR, k)
    shared_span(P_FAR, 2, 4, 5)
    total[pl.ds(368, 656)] += product_of(a_late, (368, 656))
    for k in (0, 2):
        arrived(b_links, P_FAR, k)
    add(b_late, (384, 640), (128, 384))
    for k in (3, 5):
        arrived(b_links, P_FAR, k)
    total[pl.ds(384, 640)] += part_of(b_late, (384, 640), (512, 128)) + part_of(
        b_late, (384, 640), (768, 256)
    )
    patterns[2].wait()
    shared_span(P_FAR, 0, 1, 3)
    total[pl.ds(0, 368)] += product_of(a_late, (0, 368))
    for k in (1, 4, 6):
        arrived(b_links, P_FAR, k)
    finish((0, 384), product_of(b_late, (0, 384)))
    finish(
        (384, 640),
        part_of(b_late, (384, 640), (0, 128)) + part_of(b_late, (384, 640), (640, 128)),
    )
    for copy in sent[len(ringed):]:
        copy.wait_send()


def on_device(left_blocks, right_blocks, a_pattern, b_pattern, keep_mask):
    n_sends = 64
    n_parts = 8 * PER_ORIGIN
    pattern = pltpu.SMEM(keep_mask.T.shape, jnp.int32)
    return pl.pallas_call(
        kernel,
        out_shape=jax.ShapeDtypeStruct((ROWS, COLS), jnp.bfloat16),
        in_specs=[pl.BlockSpec(memory_space=pltpu.HBM)] * 5,
        out_specs=pl.BlockSpec(memory_space=pltpu.VMEM),
        scratch_shapes=[
            pltpu.VMEM((8, 2, ROWS, COLS), jnp.bfloat16),
            pltpu.VMEM((8, ROWS, COLS), jnp.bfloat16),
            pltpu.VMEM((ROWS, COLS), jnp.float32),
            pattern,
            pattern,
            pattern,
            pltpu.SemaphoreType.DMA((2, PIECES)),
            pltpu.SemaphoreType.DMA((3,)),
            pltpu.SemaphoreType.DMA((n_sends,)),
            pltpu.SemaphoreType.DMA((n_parts,)),
            pltpu.SemaphoreType.DMA((n_sends,)),
            pltpu.SemaphoreType.DMA((n_parts,)),
            pltpu.SemaphoreType.DMA((n_sends,)),
            pltpu.SemaphoreType.DMA((n_parts,)),
        ],
        compiler_params=pltpu.CompilerParams(
            collective_id=0,
            has_side_effects=True,
            vmem_limit_bytes=40 * 1024 * 1024,
        ),
    )(*[pltpu.with_memory_space_constraint(v, pltpu.HBM) for v in (left_blocks, right_blocks, a_pattern.T, b_pattern.T, keep_mask.T)])


def solution(mesh):
    placed = (P("row", "col"),) * 5
    return jax.shard_map(
        on_device, mesh=mesh, in_specs=placed, out_specs=P("row", "col"), check_vma=False
    )
```

```python
import jax
import jax.numpy as jnp
from jax import lax
from jax.experimental import pallas as pl
from jax.experimental.pallas import tpu as pltpu
from jax.sharding import PartitionSpec as P

MESH = pl.DeviceIdType.MESH
BLOCK = 128
ROWS = 1024
COLS = 512
PIECES = 4
PIECE = ROWS // PIECES
HALF = PIECES // 2

OWN, LEFT, RIGHT, FAR, P_OWN, P_LEFT, P_RIGHT, P_FAR = range(8)
RING_STEP = (0, 3, 1, 2, 0, 3, 1, 2)

A_FAR = (
    ((0, 96), (96, 128)),
    ((352, 96), (224, 128)),
    ((448, 288), (736, 288)),
)
B_FAR = (
    ((128, 224), (0, 128)),
    ((352, 160), (512, 128), (640, 64)),
    ((768, 256), (704, 64)),
)
PER_ORIGIN = 8
ALL = (0, ROWS)


def kernel(
    left_in, right_in, a_pat_in, b_pat_in, keep_in, out,
    a_all, b_all, total, a_pat, b_pat, keep,
    load_sem, pat_sem, a_send, a_recv, b_send, b_recv, c_send, c_recv,
):
    row = lax.axis_index("row")
    col = lax.axis_index("col")
    x = row // 2
    y_lo = row % 2
    z = col // 4
    y_hi = col // 2 % 2
    core = col % 2

    x_up = ((x + 1) % 4 * 2 + y_lo, col)
    x_down = ((x + 3) % 4 * 2 + y_lo, col)
    b_plane = (x * 2 + 1 - y_lo, col)
    z_up = (row, (z + 1) % 4 * 4 + col % 4)
    z_down = (row, (z + 3) % 4 * 4 + col % 4)
    a_plane = (row, z * 4 + (1 - y_hi) * 2 + core)
    sibling = (row, col // 2 * 2 + 1 - core)

    def a_chunk(origin):
        plane = y_hi if origin < P_OWN else 1 - y_hi
        return (z + RING_STEP[origin]) % 4 * 2 + plane

    def b_chunk(origin):
        plane = y_lo if origin < P_OWN else 1 - y_lo
        return (x + RING_STEP[origin]) % 4 * 2 + plane

    barrier = pltpu.get_barrier_semaphore()
    partners = (x_up, x_down, b_plane, z_up, z_down, a_plane, sibling)
    for partner in partners:
        pl.semaphore_signal(barrier, inc=1, device_id=partner, device_id_type=MESH)

    a_own, b_own = a_chunk(OWN), b_chunk(OWN)
    patterns = [
        pltpu.make_async_copy(source, held, pat_sem.at[i])
        for i, (source, held) in enumerate(
            ((b_pat_in, b_pat), (a_pat_in, a_pat), (keep_in, keep))
        )
    ]
    for copy in patterns:
        copy.start()
    loads = []
    for i in range(PIECES):
        rows = pl.ds(i * PIECE, PIECE)
        for which, (source, held) in enumerate(
            ((right_in, b_all.at[b_own]), (left_in, a_all.at[a_own, core]))
        ):
            load = pltpu.make_async_copy(
                source.at[rows], held.at[rows], load_sem.at[which, i]
            )
            load.start()
            loads.append(load)

    def mask(held, pattern, i):
        for bi in range(i * PIECE // BLOCK, (i + 1) * PIECE // BLOCK):
            for bj in range(COLS // BLOCK):
                cells = (pl.ds(bi * BLOCK, BLOCK), pl.ds(bj * BLOCK, BLOCK))
                stored = jnp.full((BLOCK, BLOCK), pattern[bj, bi].astype(jnp.float32))
                held[cells] = held[cells] * stored.astype(jnp.bfloat16)

    sent = []

    class Stream:
        def __init__(self, slot_of, far, send_sem, recv_sem):
            self.slot_of, self.far = slot_of, far[0] + far[1] + far[2]
            self.n_up, self.n_down = len(far[0]), len(far[1])
            self.forwarded = 0
            self.send_sem, self.recv_sem = send_sem, recv_sem
            self.count = 0

        def spans(self, origin):
            if origin == P_FAR:
                return self.far
            return tuple((i * PIECE, PIECE) for i in range(PIECES))

        def send(self, origin, span, to, arrives_as, index):
            ref = self.slot_of(origin).at[pl.ds(*span)]
            copy = pltpu.make_async_remote_copy(
                src_ref=ref,
                dst_ref=ref,
                send_sem=self.send_sem.at[self.count],
                recv_sem=self.recv_sem.at[arrives_as * PER_ORIGIN + index],
                device_id=to,
                device_id_type=MESH,
            )
            self.count += 1
            copy.start()
            sent.append(copy)

        def wait(self, origin, index):
            ref = self.slot_of(origin).at[pl.ds(*self.spans(origin)[index])]
            pltpu.make_async_remote_copy(
                src_ref=ref,
                dst_ref=ref,
                send_sem=self.send_sem.at[0],
                recv_sem=self.recv_sem.at[origin * PER_ORIGIN + index],
                device_id=sibling,
                device_id_type=MESH,
            ).wait_recv()

    a_stream = Stream(lambda o: a_all.at[a_chunk(o), core], A_FAR, a_send, a_recv)
    b_stream = Stream(lambda o: b_all.at[b_chunk(o)], B_FAR, b_send, b_recv)
    c_stream = Stream(lambda o: a_all.at[a_chunk(o), core], A_FAR, c_send, c_recv)
    c_wait = Stream(lambda o: a_all.at[a_chunk(o), 1 - core], A_FAR, c_send, c_recv)

    a_links = (a_stream, z_up, z_down, a_plane)
    b_links = (b_stream, x_up, x_down, b_plane)
    both = (a_links, b_links)

    def share(origin, index):
        c_stream.send(origin, a_stream.spans(origin)[index], sibling, origin, index)

    def arrived(links, origin, index):
        stream = links[0]
        stream.wait(origin, index)
        if stream is a_stream:
            share(origin, index)

    def shared(*origins):
        for origin in origins:
            for index in range(len(a_stream.spans(origin))):
                c_wait.wait(origin, index)

    def shared_span(origin, *indices):
        for index in indices:
            c_wait.wait(origin, index)

    def send_own(links, i):
        stream, up, down, plane = links
        span = stream.spans(OWN)[i]
        stream.send(OWN, span, up, LEFT, i)
        stream.send(OWN, span, down, RIGHT, i)
        stream.send(OWN, span, plane, P_OWN, i)
        if stream is a_stream:
            share(OWN, i)

    def ring_step(links, i):
        stream, up, down, _ = links
        arrived(links, LEFT, i)
        if i < HALF:
            stream.send(LEFT, stream.spans(LEFT)[i], up, FAR, i)
        arrived(links, RIGHT, i)
        if i >= HALF:
            stream.send(RIGHT, stream.spans(RIGHT)[i], down, FAR, i)

    def plane_step(links, i):
        stream, up, down, _ = links
        arrived(links, P_OWN, i)
        span = stream.spans(P_OWN)[i]
        stream.send(P_OWN, span, up, P_LEFT, i)
        stream.send(P_OWN, span, down, P_RIGHT, i)

    def forward(links, origin, to, first, stop, i):
        stream = links[0]
        covered = [span[0] + span[1] <= (i + 1) * PIECE for span in stream.far[first:stop]]
        before = [span[0] + span[1] <= i * PIECE for span in stream.far[first:stop]]
        if all(covered) and not all(before):
            for k in range(first, stop):
                stream.send(origin, stream.far[k], to, P_FAR, k)

    def partner_ring_step(links, i):
        stream, up, down, _ = links
        n_up, n_down = stream.n_up, stream.n_down
        arrived(links, P_LEFT, i)
        forward(links, P_LEFT, up, 0, n_up, i)
        arrived(links, P_RIGHT, i)
        forward(links, P_RIGHT, down, n_up, n_up + n_down, i)

    def plane_far(links):
        stream, plane = links[0], links[3]
        for k in range(stream.n_up + stream.n_down, len(stream.far)):
            stream.send(FAR, stream.far[k], plane, P_FAR, k)

    def part_of(chunk, rows, depth):
        cells = pl.ds(*rows)
        first, count = depth
        half, start = first // COLS, first % COLS
        return jnp.dot(
            a_all[chunk, half, cells, start : start + count],
            b_all[chunk, first : first + count],
            preferred_element_type=jnp.float32,
        )

    def add(chunk, rows, depth):
        total[pl.ds(*rows)] += part_of(chunk, rows, depth)

    def product_of(chunk, rows):
        cells = pl.ds(*rows)
        return jnp.dot(
            a_all[chunk, 0, cells], b_all[chunk, 0:COLS],
            preferred_element_type=jnp.float32,
        ) + jnp.dot(
            a_all[chunk, 1, cells], b_all[chunk, COLS:ROWS],
            preferred_element_type=jnp.float32,
        )

    def finish(rows, added):
        first, count = rows
        result = total[pl.ds(*rows)] + added
        for bi in range(count // BLOCK):
            for bj in range(COLS // BLOCK):
                kept = keep[bj, first // BLOCK + bi].astype(jnp.float32)
                block = result[
                    bi * BLOCK : (bi + 1) * BLOCK, bj * BLOCK : (bj + 1) * BLOCK
                ]
                out[
                    pl.ds(first + bi * BLOCK, BLOCK), pl.ds(bj * BLOCK, BLOCK)
                ] = (block * kept).astype(jnp.bfloat16)

    meet = 1 - (y_hi + y_lo) % 2
    turn = (x + 4 - z) % 4
    odd = turn % 2
    turned = (turn + 3) // 4

    def choose(if_meet, otherwise):
        return meet * if_meet + (1 - meet) * otherwise

    def partner_chunk(step):
        return (z + step) % 4 * 2 + 1 - y_hi

    early = (
        choose(a_chunk(OWN), b_chunk(P_OWN)),
        choose(a_chunk(FAR), a_chunk(P_OWN)),
    )
    middle = (
        choose(a_chunk(LEFT), b_chunk(P_LEFT)),
        choose(a_chunk(RIGHT), b_chunk(P_RIGHT)),
        choose(partner_chunk(1 - odd), a_chunk(P_LEFT)),
        choose(partner_chunk((1 - odd) * 3 + odd * turn), a_chunk(P_RIGHT)),
    )
    a_late = choose(partner_chunk(2 * turned), a_chunk(P_FAR))
    b_late = b_chunk(P_FAR)

    for copy in patterns[:2]:
        copy.wait()
    for i in range(PIECES):
        loads[2 * i + 1].wait()
        mask(a_all.at[a_own, core], a_pat, i)
        if i == 0:
            pl.semaphore_wait(barrier, len(partners))
        send_own(a_links, i)
        loads[2 * i].wait()
        mask(b_all.at[b_own], b_pat, i)
        send_own(b_links, i)

    for i in range(PIECES):
        for links in both:
            ring_step(links, i)
    for i in range(PIECES - 1):
        for links in both:
            plane_step(links, i)
    for i, j in ((0, HALF), (HALF - 1, PIECES - 1)):
        for links in both:
            for index in dict.fromkeys((i, j)):
                arrived(links, FAR, index)
    for links in both:
        plane_far(links)
    for links in both:
        plane_step(links, PIECES - 1)
    shared(OWN, LEFT, RIGHT, FAR, P_OWN)
    total[...] = product_of(early[0], ALL)
    for links in both:
        partner_ring_step(links, 0)
    total[...] += product_of(early[1], ALL)
    for links in both:
        partner_ring_step(links, 1)
    add(middle[0], ALL, (0, 512))
    add(middle[1], ALL, (0, 512))
    shared_span(P_LEFT, 0, 1)
    shared_span(P_RIGHT, 0, 1)
    add(middle[2], (0, 512), (0, 512))
    add(middle[3], (0, 512), (0, 512))
    for links in both:
        partner_ring_step(links, 2)
    add(middle[0], ALL, (512, 256))
    add(middle[1], ALL, (512, 256))
    for links in both:
        partner_ring_step(links, 3)
    add(middle[0], ALL, (768, 256))
    add(middle[1], ALL, (768, 256))
    shared_span(P_LEFT, 2, 3)
    shared_span(P_RIGHT, 2, 3)
    add(middle[2], (512, 512), (0, 512))
    add(middle[3], (512, 512), (0, 512))
    ringed = list(sent)
    for k in (4, 5):
        arrived(a_links, P_FAR, k)
    add(middle[2], ALL, (512, 512))
    for k in (0, 2):
        arrived(a_links, P_FAR, k)
    add(middle[3], ALL, (512, 512))
    for copy in ringed:
        copy.wait_send()
    for k in (1, 3):
        arrived(a_links, P_FAR, k)
    shared_span(P_FAR, 2, 4, 5)
    total[pl.ds(352, 672)] += product_of(a_late, (352, 672))
    for k in (0, 2):
        arrived(b_links, P_FAR, k)
    add(b_late, (384, 640), (128, 384))
    for k in (3, 5):
        arrived(b_links, P_FAR, k)
    total[pl.ds(384, 640)] += part_of(b_late, (384, 640), (512, 128)) + part_of(
        b_late, (384, 640), (768, 256)
    )
    patterns[2].wait()
    shared_span(P_FAR, 0, 1, 3)
    total[pl.ds(0, 352)] += product_of(a_late, (0, 352))
    for k in (1, 4, 6):
        arrived(b_links, P_FAR, k)
    finish((0, 384), product_of(b_late, (0, 384)))
    finish(
        (384, 640),
        part_of(b_late, (384, 640), (0, 128)) + part_of(b_late, (384, 640), (640, 128)),
    )
    for copy in sent[len(ringed):]:
        copy.wait_send()


def on_device(left_blocks, right_blocks, a_pattern, b_pattern, keep_mask):
    n_sends = 64
    n_parts = 8 * PER_ORIGIN
    pattern = pltpu.SMEM(keep_mask.T.shape, jnp.int32)
    return pl.pallas_call(
        kernel,
        out_shape=jax.ShapeDtypeStruct((ROWS, COLS), jnp.bfloat16),
        in_specs=[pl.BlockSpec(memory_space=pltpu.HBM)] * 5,
        out_specs=pl.BlockSpec(memory_space=pltpu.VMEM),
        scratch_shapes=[
            pltpu.VMEM((8, 2, ROWS, COLS), jnp.bfloat16),
            pltpu.VMEM((8, ROWS, COLS), jnp.bfloat16),
            pltpu.VMEM((ROWS, COLS), jnp.float32),
            pattern,
            pattern,
            pattern,
            pltpu.SemaphoreType.DMA((2, PIECES)),
            pltpu.SemaphoreType.DMA((3,)),
            pltpu.SemaphoreType.DMA((n_sends,)),
            pltpu.SemaphoreType.DMA((n_parts,)),
            pltpu.SemaphoreType.DMA((n_sends,)),
            pltpu.SemaphoreType.DMA((n_parts,)),
            pltpu.SemaphoreType.DMA((n_sends,)),
            pltpu.SemaphoreType.DMA((n_parts,)),
        ],
        compiler_params=pltpu.CompilerParams(
            collective_id=0,
            has_side_effects=True,
            vmem_limit_bytes=40 * 1024 * 1024,
        ),
    )(*[pltpu.with_memory_space_constraint(v, pltpu.HBM) for v in (left_blocks, right_blocks, a_pattern.T, b_pattern.T, keep_mask.T)])


def solution(mesh):
    placed = (P("row", "col"),) * 5
    return jax.shard_map(
        on_device, mesh=mesh, in_specs=placed, out_specs=P("row", "col"), check_vma=False
    )
```

```python
import jax
import jax.numpy as jnp
from jax import lax
from jax.experimental import pallas as pl
from jax.experimental.pallas import tpu as pltpu
from jax.sharding import PartitionSpec as P

MESH = pl.DeviceIdType.MESH
BLOCK = 128
ROWS = 1024
COLS = 512
PIECES = 4
PIECE = ROWS // PIECES
HALF = PIECES // 2

OWN, LEFT, RIGHT, FAR, P_OWN, P_LEFT, P_RIGHT, P_FAR = range(8)
RING_STEP = (0, 3, 1, 2, 0, 3, 1, 2)

A_FAR = (
    ((0, 96), (96, 128)),
    ((352, 96), (224, 128)),
    ((448, 288), (736, 288)),
)
B_FAR = (
    ((128, 224), (0, 128)),
    ((352, 160), (512, 128), (640, 64)),
    ((768, 256), (704, 64)),
)
PER_ORIGIN = 8
ALL = (0, ROWS)


def kernel(
    left_in, right_in, a_pat_in, b_pat_in, keep_in, out,
    a_all, b_all, total, a_pat, b_pat, keep,
    load_sem, pat_sem, a_send, a_recv, b_send, b_recv, c_send, c_recv,
):
    row = lax.axis_index("row")
    col = lax.axis_index("col")
    x = row // 2
    y_lo = row % 2
    z = col // 4
    y_hi = col // 2 % 2
    core = col % 2

    x_up = ((x + 1) % 4 * 2 + y_lo, col)
    x_down = ((x + 3) % 4 * 2 + y_lo, col)
    b_plane = (x * 2 + 1 - y_lo, col)
    z_up = (row, (z + 1) % 4 * 4 + col % 4)
    z_down = (row, (z + 3) % 4 * 4 + col % 4)
    a_plane = (row, z * 4 + (1 - y_hi) * 2 + core)
    sibling = (row, col // 2 * 2 + 1 - core)

    def a_chunk(origin):
        plane = y_hi if origin < P_OWN else 1 - y_hi
        return (z + RING_STEP[origin]) % 4 * 2 + plane

    def b_chunk(origin):
        plane = y_lo if origin < P_OWN else 1 - y_lo
        return (x + RING_STEP[origin]) % 4 * 2 + plane

    barrier = pltpu.get_barrier_semaphore()
    partners = (x_up, x_down, b_plane, z_up, z_down, a_plane, sibling)
    for partner in partners:
        pl.semaphore_signal(barrier, inc=1, device_id=partner, device_id_type=MESH)

    a_own, b_own = a_chunk(OWN), b_chunk(OWN)
    patterns = [
        pltpu.make_async_copy(source, held, pat_sem.at[i])
        for i, (source, held) in enumerate(
            ((b_pat_in, b_pat), (a_pat_in, a_pat), (keep_in, keep))
        )
    ]
    for copy in patterns:
        copy.start()
    loads = []
    for i in range(PIECES):
        rows = pl.ds(i * PIECE, PIECE)
        for which, (source, held) in enumerate(
            ((right_in, b_all.at[b_own]), (left_in, a_all.at[a_own, core]))
        ):
            load = pltpu.make_async_copy(
                source.at[rows], held.at[rows], load_sem.at[which, i]
            )
            load.start()
            loads.append(load)

    def mask(held, pattern, i):
        for bi in range(i * PIECE // BLOCK, (i + 1) * PIECE // BLOCK):
            for bj in range(COLS // BLOCK):
                cells = (pl.ds(bi * BLOCK, BLOCK), pl.ds(bj * BLOCK, BLOCK))
                stored = jnp.full((BLOCK, BLOCK), pattern[bj, bi].astype(jnp.float32))
                held[cells] = held[cells] * stored.astype(jnp.bfloat16)

    sent = []

    class Stream:
        def __init__(self, slot_of, far, send_sem, recv_sem):
            self.slot_of, self.far = slot_of, far[0] + far[1] + far[2]
            self.n_up, self.n_down = len(far[0]), len(far[1])
            self.forwarded = 0
            self.send_sem, self.recv_sem = send_sem, recv_sem
            self.count = 0

        def spans(self, origin):
            if origin == P_FAR:
                return self.far
            return tuple((i * PIECE, PIECE) for i in range(PIECES))

        def send(self, origin, span, to, arrives_as, index):
            ref = self.slot_of(origin).at[pl.ds(*span)]
            copy = pltpu.make_async_remote_copy(
                src_ref=ref,
                dst_ref=ref,
                send_sem=self.send_sem.at[self.count],
                recv_sem=self.recv_sem.at[arrives_as * PER_ORIGIN + index],
                device_id=to,
                device_id_type=MESH,
            )
            self.count += 1
            copy.start()
            sent.append(copy)

        def wait(self, origin, index):
            ref = self.slot_of(origin).at[pl.ds(*self.spans(origin)[index])]
            pltpu.make_async_remote_copy(
                src_ref=ref,
                dst_ref=ref,
                send_sem=self.send_sem.at[0],
                recv_sem=self.recv_sem.at[origin * PER_ORIGIN + index],
                device_id=sibling,
                device_id_type=MESH,
            ).wait_recv()

    a_stream = Stream(lambda o: a_all.at[a_chunk(o), core], A_FAR, a_send, a_recv)
    b_stream = Stream(lambda o: b_all.at[b_chunk(o)], B_FAR, b_send, b_recv)
    c_stream = Stream(lambda o: a_all.at[a_chunk(o), core], A_FAR, c_send, c_recv)
    c_wait = Stream(lambda o: a_all.at[a_chunk(o), 1 - core], A_FAR, c_send, c_recv)

    a_links = (a_stream, z_up, z_down, a_plane)
    b_links = (b_stream, x_up, x_down, b_plane)
    both = (a_links, b_links)

    def share(origin, index):
        c_stream.send(origin, a_stream.spans(origin)[index], sibling, origin, index)

    def arrived(links, origin, index):
        stream = links[0]
        stream.wait(origin, index)
        if stream is a_stream:
            share(origin, index)

    def shared(*origins):
        for origin in origins:
            for index in range(len(a_stream.spans(origin))):
                c_wait.wait(origin, index)

    def shared_span(origin, *indices):
        for index in indices:
            c_wait.wait(origin, index)

    def send_own(links, i):
        stream, up, down, plane = links
        span = stream.spans(OWN)[i]
        stream.send(OWN, span, up, LEFT, i)
        stream.send(OWN, span, down, RIGHT, i)
        stream.send(OWN, span, plane, P_OWN, i)
        if stream is a_stream:
            share(OWN, i)

    def ring_step(links, i):
        stream, up, down, _ = links
        arrived(links, LEFT, i)
        if i < HALF:
            stream.send(LEFT, stream.spans(LEFT)[i], up, FAR, i)
        arrived(links, RIGHT, i)
        if i >= HALF:
            stream.send(RIGHT, stream.spans(RIGHT)[i], down, FAR, i)

    def plane_step(links, i):
        stream, up, down, _ = links
        arrived(links, P_OWN, i)
        span = stream.spans(P_OWN)[i]
        stream.send(P_OWN, span, up, P_LEFT, i)
        stream.send(P_OWN, span, down, P_RIGHT, i)

    def forward(links, origin, to, first, stop, i):
        stream = links[0]
        covered = [span[0] + span[1] <= (i + 1) * PIECE for span in stream.far[first:stop]]
        before = [span[0] + span[1] <= i * PIECE for span in stream.far[first:stop]]
        if all(covered) and not all(before):
            for k in range(first, stop):
                stream.send(origin, stream.far[k], to, P_FAR, k)

    def partner_ring_step(links, i):
        stream, up, down, _ = links
        n_up, n_down = stream.n_up, stream.n_down
        arrived(links, P_LEFT, i)
        forward(links, P_LEFT, up, 0, n_up, i)
        arrived(links, P_RIGHT, i)
        forward(links, P_RIGHT, down, n_up, n_up + n_down, i)

    def plane_far(links):
        stream, plane = links[0], links[3]
        for k in range(stream.n_up + stream.n_down, len(stream.far)):
            stream.send(FAR, stream.far[k], plane, P_FAR, k)

    def part_of(chunk, rows, depth):
        cells = pl.ds(*rows)
        first, count = depth
        half, start = first // COLS, first % COLS
        return jnp.dot(
            a_all[chunk, half, cells, start : start + count],
            b_all[chunk, first : first + count],
            preferred_element_type=jnp.float32,
        )

    def add(chunk, rows, depth):
        total[pl.ds(*rows)] += part_of(chunk, rows, depth)

    def product_of(chunk, rows):
        cells = pl.ds(*rows)
        return jnp.dot(
            a_all[chunk, 0, cells], b_all[chunk, 0:COLS],
            preferred_element_type=jnp.float32,
        ) + jnp.dot(
            a_all[chunk, 1, cells], b_all[chunk, COLS:ROWS],
            preferred_element_type=jnp.float32,
        )

    def finish(rows, added):
        first, count = rows
        result = total[pl.ds(*rows)] + added
        for bi in range(count // BLOCK):
            for bj in range(COLS // BLOCK):
                kept = keep[bj, first // BLOCK + bi].astype(jnp.float32)
                block = result[
                    bi * BLOCK : (bi + 1) * BLOCK, bj * BLOCK : (bj + 1) * BLOCK
                ]
                out[
                    pl.ds(first + bi * BLOCK, BLOCK), pl.ds(bj * BLOCK, BLOCK)
                ] = (block * kept).astype(jnp.bfloat16)

    meet = 1 - (y_hi + y_lo) % 2
    turn = (x + 4 - z) % 4
    odd = turn % 2
    turned = (turn + 3) // 4

    def choose(if_meet, otherwise):
        return meet * if_meet + (1 - meet) * otherwise

    def partner_chunk(step):
        return (z + step) % 4 * 2 + 1 - y_hi

    early = (
        choose(a_chunk(OWN), b_chunk(P_OWN)),
        choose(a_chunk(FAR), a_chunk(P_OWN)),
    )
    middle = (
        choose(a_chunk(LEFT), b_chunk(P_LEFT)),
        choose(a_chunk(RIGHT), b_chunk(P_RIGHT)),
        choose(partner_chunk(1 - odd), a_chunk(P_LEFT)),
        choose(partner_chunk((1 - odd) * 3 + odd * turn), a_chunk(P_RIGHT)),
    )
    a_late = choose(partner_chunk(2 * turned), a_chunk(P_FAR))
    b_late = b_chunk(P_FAR)

    for copy in patterns[:2]:
        copy.wait()
    for i in range(PIECES):
        loads[2 * i + 1].wait()
        mask(a_all.at[a_own, core], a_pat, i)
        if i == 0:
            pl.semaphore_wait(barrier, len(partners))
        send_own(a_links, i)
        loads[2 * i].wait()
        mask(b_all.at[b_own], b_pat, i)
        send_own(b_links, i)

    for i in range(PIECES):
        for links in both:
            ring_step(links, i)
    for i in range(PIECES - 1):
        for links in both:
            plane_step(links, i)
    for i, j in ((0, HALF), (HALF - 1, PIECES - 1)):
        for links in both:
            for index in dict.fromkeys((i, j)):
                arrived(links, FAR, index)
    for links in both:
        plane_far(links)
    for links in both:
        plane_step(links, PIECES - 1)
    shared(OWN, LEFT, RIGHT, FAR, P_OWN)
    total[...] = product_of(early[0], ALL)
    for links in both:
        partner_ring_step(links, 0)
    total[...] += product_of(early[1], ALL)
    for links in both:
        partner_ring_step(links, 1)
    add(middle[0], ALL, (0, 512))
    add(middle[1], ALL, (0, 512))
    shared_span(P_LEFT, 0, 1)
    shared_span(P_RIGHT, 0, 1)
    add(middle[2], (0, 512), (0, 512))
    add(middle[3], (0, 512), (0, 512))
    for links in both:
        partner_ring_step(links, 2)
    add(middle[0], ALL, (512, 256))
    add(middle[1], ALL, (512, 256))
    for links in both:
        partner_ring_step(links, 3)
    add(middle[0], ALL, (768, 256))
    add(middle[1], ALL, (768, 256))
    shared_span(P_LEFT, 2, 3)
    shared_span(P_RIGHT, 2, 3)
    add(middle[2], (512, 512), (0, 512))
    add(middle[3], (512, 512), (0, 512))
    ringed = list(sent)
    for k in (4, 5):
        arrived(a_links, P_FAR, k)
    add(middle[2], ALL, (512, 512))
    for k in (0, 2):
        arrived(a_links, P_FAR, k)
    add(middle[3], ALL, (512, 512))
    for copy in ringed:
        copy.wait_send()
    for k in (1, 3):
        arrived(a_links, P_FAR, k)
    shared_span(P_FAR, 2, 4, 5)
    total[pl.ds(384, 640)] += product_of(a_late, (384, 640))
    for k in (0, 2):
        arrived(b_links, P_FAR, k)
    add(b_late, (384, 640), (128, 384))
    for k in (3, 5):
        arrived(b_links, P_FAR, k)
    total[pl.ds(384, 640)] += part_of(b_late, (384, 640), (512, 128)) + part_of(
        b_late, (384, 640), (768, 256)
    )
    patterns[2].wait()
    shared_span(P_FAR, 0, 1, 3)
    for k in (1, 4, 6):
        arrived(b_links, P_FAR, k)
    finish((0, 384), product_of(a_late, (0, 384)) + product_of(b_late, (0, 384)))
    finish(
        (384, 640),
        part_of(b_late, (384, 640), (0, 128)) + part_of(b_late, (384, 640), (640, 128)),
    )
    for copy in sent[len(ringed):]:
        copy.wait_send()


def on_device(left_blocks, right_blocks, a_pattern, b_pattern, keep_mask):
    n_sends = 64
    n_parts = 8 * PER_ORIGIN
    pattern = pltpu.SMEM(keep_mask.T.shape, jnp.int32)
    return pl.pallas_call(
        kernel,
        out_shape=jax.ShapeDtypeStruct((ROWS, COLS), jnp.bfloat16),
        in_specs=[pl.BlockSpec(memory_space=pltpu.HBM)] * 5,
        out_specs=pl.BlockSpec(memory_space=pltpu.VMEM),
        scratch_shapes=[
            pltpu.VMEM((8, 2, ROWS, COLS), jnp.bfloat16),
            pltpu.VMEM((8, ROWS, COLS), jnp.bfloat16),
            pltpu.VMEM((ROWS, COLS), jnp.float32),
            pattern,
            pattern,
            pattern,
            pltpu.SemaphoreType.DMA((2, PIECES)),
            pltpu.SemaphoreType.DMA((3,)),
            pltpu.SemaphoreType.DMA((n_sends,)),
            pltpu.SemaphoreType.DMA((n_parts,)),
            pltpu.SemaphoreType.DMA((n_sends,)),
            pltpu.SemaphoreType.DMA((n_parts,)),
            pltpu.SemaphoreType.DMA((n_sends,)),
            pltpu.SemaphoreType.DMA((n_parts,)),
        ],
        compiler_params=pltpu.CompilerParams(
            collective_id=0,
            has_side_effects=True,
            vmem_limit_bytes=40 * 1024 * 1024,
        ),
    )(*[pltpu.with_memory_space_constraint(v, pltpu.HBM) for v in (left_blocks, right_blocks, a_pattern.T, b_pattern.T, keep_mask.T)])


def solution(mesh):
    placed = (P("row", "col"),) * 5
    return jax.shard_map(
        on_device, mesh=mesh, in_specs=placed, out_specs=P("row", "col"), check_vma=False
    )
```

```python
import jax
import jax.numpy as jnp
from jax import lax
from jax.experimental import pallas as pl
from jax.experimental.pallas import tpu as pltpu
from jax.sharding import PartitionSpec as P

MESH = pl.DeviceIdType.MESH
BLOCK = 128
ROWS = 1024
COLS = 512
PIECES = 4
PIECE = ROWS // PIECES
HALF = PIECES // 2

OWN, LEFT, RIGHT, FAR, P_OWN, P_LEFT, P_RIGHT, P_FAR = range(8)
RING_STEP = (0, 3, 1, 2, 0, 3, 1, 2)

A_FAR = (
    ((0, 96), (96, 128)),
    ((352, 96), (224, 128)),
    ((448, 288), (736, 288)),
)
B_FAR = (
    ((128, 208), (0, 128)),
    ((336, 176), (512, 128), (640, 32)),
    ((768, 256), (672, 96)),
)
PER_ORIGIN = 8
ALL = (0, ROWS)


def kernel(
    left_in, right_in, a_pat_in, b_pat_in, keep_in, out,
    a_all, b_all, total, a_pat, b_pat, keep,
    load_sem, pat_sem, a_send, a_recv, b_send, b_recv, c_send, c_recv,
):
    row = lax.axis_index("row")
    col = lax.axis_index("col")
    x = row // 2
    y_lo = row % 2
    z = col // 4
    y_hi = col // 2 % 2
    core = col % 2

    x_up = ((x + 1) % 4 * 2 + y_lo, col)
    x_down = ((x + 3) % 4 * 2 + y_lo, col)
    b_plane = (x * 2 + 1 - y_lo, col)
    z_up = (row, (z + 1) % 4 * 4 + col % 4)
    z_down = (row, (z + 3) % 4 * 4 + col % 4)
    a_plane = (row, z * 4 + (1 - y_hi) * 2 + core)
    sibling = (row, col // 2 * 2 + 1 - core)

    def a_chunk(origin):
        plane = y_hi if origin < P_OWN else 1 - y_hi
        return (z + RING_STEP[origin]) % 4 * 2 + plane

    def b_chunk(origin):
        plane = y_lo if origin < P_OWN else 1 - y_lo
        return (x + RING_STEP[origin]) % 4 * 2 + plane

    barrier = pltpu.get_barrier_semaphore()
    partners = (x_up, x_down, b_plane, z_up, z_down, a_plane, sibling)
    for partner in partners:
        pl.semaphore_signal(barrier, inc=1, device_id=partner, device_id_type=MESH)

    a_own, b_own = a_chunk(OWN), b_chunk(OWN)
    patterns = [
        pltpu.make_async_copy(source, held, pat_sem.at[i])
        for i, (source, held) in enumerate(
            ((b_pat_in, b_pat), (a_pat_in, a_pat), (keep_in, keep))
        )
    ]
    for copy in patterns:
        copy.start()
    loads = []
    for i in range(PIECES):
        rows = pl.ds(i * PIECE, PIECE)
        for which, (source, held) in enumerate(
            ((right_in, b_all.at[b_own]), (left_in, a_all.at[a_own, core]))
        ):
            load = pltpu.make_async_copy(
                source.at[rows], held.at[rows], load_sem.at[which, i]
            )
            load.start()
            loads.append(load)

    def mask(held, pattern, i):
        for bi in range(i * PIECE // BLOCK, (i + 1) * PIECE // BLOCK):
            for bj in range(COLS // BLOCK):
                cells = (pl.ds(bi * BLOCK, BLOCK), pl.ds(bj * BLOCK, BLOCK))
                stored = jnp.full((BLOCK, BLOCK), pattern[bj, bi].astype(jnp.float32))
                held[cells] = held[cells] * stored.astype(jnp.bfloat16)

    sent = []

    class Stream:
        def __init__(self, slot_of, far, send_sem, recv_sem):
            self.slot_of, self.far = slot_of, far[0] + far[1] + far[2]
            self.n_up, self.n_down = len(far[0]), len(far[1])
            self.forwarded = 0
            self.send_sem, self.recv_sem = send_sem, recv_sem
            self.count = 0

        def spans(self, origin):
            if origin == P_FAR:
                return self.far
            return tuple((i * PIECE, PIECE) for i in range(PIECES))

        def send(self, origin, span, to, arrives_as, index):
            ref = self.slot_of(origin).at[pl.ds(*span)]
            copy = pltpu.make_async_remote_copy(
                src_ref=ref,
                dst_ref=ref,
                send_sem=self.send_sem.at[self.count],
                recv_sem=self.recv_sem.at[arrives_as * PER_ORIGIN + index],
                device_id=to,
                device_id_type=MESH,
            )
            self.count += 1
            copy.start()
            sent.append(copy)

        def wait(self, origin, index):
            ref = self.slot_of(origin).at[pl.ds(*self.spans(origin)[index])]
            pltpu.make_async_remote_copy(
                src_ref=ref,
                dst_ref=ref,
                send_sem=self.send_sem.at[0],
                recv_sem=self.recv_sem.at[origin * PER_ORIGIN + index],
                device_id=sibling,
                device_id_type=MESH,
            ).wait_recv()

    a_stream = Stream(lambda o: a_all.at[a_chunk(o), core], A_FAR, a_send, a_recv)
    b_stream = Stream(lambda o: b_all.at[b_chunk(o)], B_FAR, b_send, b_recv)
    c_stream = Stream(lambda o: a_all.at[a_chunk(o), core], A_FAR, c_send, c_recv)
    c_wait = Stream(lambda o: a_all.at[a_chunk(o), 1 - core], A_FAR, c_send, c_recv)

    a_links = (a_stream, z_up, z_down, a_plane)
    b_links = (b_stream, x_up, x_down, b_plane)
    both = (a_links, b_links)

    def share(origin, index):
        c_stream.send(origin, a_stream.spans(origin)[index], sibling, origin, index)

    def arrived(links, origin, index):
        stream = links[0]
        stream.wait(origin, index)
        if stream is a_stream:
            share(origin, index)

    def shared(*origins):
        for origin in origins:
            for index in range(len(a_stream.spans(origin))):
                c_wait.wait(origin, index)

    def shared_span(origin, *indices):
        for index in indices:
            c_wait.wait(origin, index)

    def send_own(links, i):
        stream, up, down, plane = links
        span = stream.spans(OWN)[i]
        stream.send(OWN, span, up, LEFT, i)
        stream.send(OWN, span, down, RIGHT, i)
        stream.send(OWN, span, plane, P_OWN, i)
        if stream is a_stream:
            share(OWN, i)

    def ring_step(links, i):
        stream, up, down, _ = links
        arrived(links, LEFT, i)
        if i < HALF:
            stream.send(LEFT, stream.spans(LEFT)[i], up, FAR, i)
        arrived(links, RIGHT, i)
        if i >= HALF:
            stream.send(RIGHT, stream.spans(RIGHT)[i], down, FAR, i)

    def plane_step(links, i):
        stream, up, down, _ = links
        arrived(links, P_OWN, i)
        span = stream.spans(P_OWN)[i]
        stream.send(P_OWN, span, up, P_LEFT, i)
        stream.send(P_OWN, span, down, P_RIGHT, i)

    def forward(links, origin, to, first, stop, i):
        stream = links[0]
        covered = [span[0] + span[1] <= (i + 1) * PIECE for span in stream.far[first:stop]]
        before = [span[0] + span[1] <= i * PIECE for span in stream.far[first:stop]]
        if all(covered) and not all(before):
            for k in range(first, stop):
                stream.send(origin, stream.far[k], to, P_FAR, k)

    def partner_ring_step(links, i):
        stream, up, down, _ = links
        n_up, n_down = stream.n_up, stream.n_down
        arrived(links, P_LEFT, i)
        forward(links, P_LEFT, up, 0, n_up, i)
        arrived(links, P_RIGHT, i)
        forward(links, P_RIGHT, down, n_up, n_up + n_down, i)

    def plane_far(links):
        stream, plane = links[0], links[3]
        for k in range(stream.n_up + stream.n_down, len(stream.far)):
            stream.send(FAR, stream.far[k], plane, P_FAR, k)

    def part_of(chunk, rows, depth):
        cells = pl.ds(*rows)
        first, count = depth
        half, start = first // COLS, first % COLS
        return jnp.dot(
            a_all[chunk, half, cells, start : start + count],
            b_all[chunk, first : first + count],
            preferred_element_type=jnp.float32,
        )

    def add(chunk, rows, depth):
        total[pl.ds(*rows)] += part_of(chunk, rows, depth)

    def product_of(chunk, rows):
        cells = pl.ds(*rows)
        return jnp.dot(
            a_all[chunk, 0, cells], b_all[chunk, 0:COLS],
            preferred_element_type=jnp.float32,
        ) + jnp.dot(
            a_all[chunk, 1, cells], b_all[chunk, COLS:ROWS],
            preferred_element_type=jnp.float32,
        )

    def finish(rows, added):
        first, count = rows
        result = total[pl.ds(*rows)] + added
        for bi in range(count // BLOCK):
            for bj in range(COLS // BLOCK):
                kept = keep[bj, first // BLOCK + bi].astype(jnp.float32)
                block = result[
                    bi * BLOCK : (bi + 1) * BLOCK, bj * BLOCK : (bj + 1) * BLOCK
                ]
                out[
                    pl.ds(first + bi * BLOCK, BLOCK), pl.ds(bj * BLOCK, BLOCK)
                ] = (block * kept).astype(jnp.bfloat16)

    meet = 1 - (y_hi + y_lo) % 2
    turn = (x + 4 - z) % 4
    odd = turn % 2
    turned = (turn + 3) // 4

    def choose(if_meet, otherwise):
        return meet * if_meet + (1 - meet) * otherwise

    def partner_chunk(step):
        return (z + step) % 4 * 2 + 1 - y_hi

    early = (
        choose(a_chunk(OWN), b_chunk(P_OWN)),
        choose(a_chunk(FAR), a_chunk(P_OWN)),
    )
    middle = (
        choose(a_chunk(LEFT), b_chunk(P_LEFT)),
        choose(a_chunk(RIGHT), b_chunk(P_RIGHT)),
        choose(partner_chunk(1 - odd), a_chunk(P_LEFT)),
        choose(partner_chunk((1 - odd) * 3 + odd * turn), a_chunk(P_RIGHT)),
    )
    a_late = choose(partner_chunk(2 * turned), a_chunk(P_FAR))
    b_late = b_chunk(P_FAR)

    for copy in patterns[:2]:
        copy.wait()
    for i in range(PIECES):
        loads[2 * i + 1].wait()
        mask(a_all.at[a_own, core], a_pat, i)
        if i == 0:
            pl.semaphore_wait(barrier, len(partners))
        send_own(a_links, i)
        loads[2 * i].wait()
        mask(b_all.at[b_own], b_pat, i)
        send_own(b_links, i)

    for i in range(PIECES):
        for links in both:
            ring_step(links, i)
    for i in range(PIECES - 1):
        for links in both:
            plane_step(links, i)
    for i, j in ((0, HALF), (HALF - 1, PIECES - 1)):
        for links in both:
            for index in dict.fromkeys((i, j)):
                arrived(links, FAR, index)
    for links in both:
        plane_far(links)
    for links in both:
        plane_step(links, PIECES - 1)
    shared(OWN, LEFT, RIGHT, FAR, P_OWN)
    total[...] = product_of(early[0], ALL)
    for links in both:
        partner_ring_step(links, 0)
    total[...] += product_of(early[1], ALL)
    for links in both:
        partner_ring_step(links, 1)
    add(middle[0], ALL, (0, 512))
    add(middle[1], ALL, (0, 512))
    shared_span(P_LEFT, 0, 1)
    shared_span(P_RIGHT, 0, 1)
    add(middle[2], (0, 512), (0, 512))
    add(middle[3], (0, 512), (0, 512))
    for links in both:
        partner_ring_step(links, 2)
    add(middle[0], ALL, (512, 256))
    add(middle[1], ALL, (512, 256))
    for links in both:
        partner_ring_step(links, 3)
    add(middle[0], ALL, (768, 256))
    add(middle[1], ALL, (768, 256))
    shared_span(P_LEFT, 2, 3)
    shared_span(P_RIGHT, 2, 3)
    add(middle[2], (512, 512), (0, 512))
    add(middle[3], (512, 512), (0, 512))
    ringed = list(sent)
    for k in (4, 5):
        arrived(a_links, P_FAR, k)
    add(middle[2], ALL, (512, 512))
    for k in (0, 2):
        arrived(a_links, P_FAR, k)
    add(middle[3], ALL, (512, 512))
    for copy in ringed:
        copy.wait_send()
    for k in (1, 3):
        arrived(a_links, P_FAR, k)
    shared_span(P_FAR, 2, 4, 5)
    total[pl.ds(384, 640)] += product_of(a_late, (384, 640))
    for k in (0, 2):
        arrived(b_links, P_FAR, k)
    add(b_late, (384, 640), (128, 384))
    for k in (3, 5):
        arrived(b_links, P_FAR, k)
    total[pl.ds(384, 640)] += part_of(b_late, (384, 640), (512, 128)) + part_of(
        b_late, (384, 640), (768, 256)
    )
    patterns[2].wait()
    shared_span(P_FAR, 0, 1, 3)
    for k in (1, 4, 6):
        arrived(b_links, P_FAR, k)
    finish((0, 384), product_of(a_late, (0, 384)) + product_of(b_late, (0, 384)))
    finish(
        (384, 640),
        part_of(b_late, (384, 640), (0, 128)) + part_of(b_late, (384, 640), (640, 128)),
    )
    for copy in sent[len(ringed):]:
        copy.wait_send()


def on_device(left_blocks, right_blocks, a_pattern, b_pattern, keep_mask):
    n_sends = 64
    n_parts = 8 * PER_ORIGIN
    pattern = pltpu.SMEM(keep_mask.T.shape, jnp.int32)
    return pl.pallas_call(
        kernel,
        out_shape=jax.ShapeDtypeStruct((ROWS, COLS), jnp.bfloat16),
        in_specs=[pl.BlockSpec(memory_space=pltpu.HBM)] * 5,
        out_specs=pl.BlockSpec(memory_space=pltpu.VMEM),
        scratch_shapes=[
            pltpu.VMEM((8, 2, ROWS, COLS), jnp.bfloat16),
            pltpu.VMEM((8, ROWS, COLS), jnp.bfloat16),
            pltpu.VMEM((ROWS, COLS), jnp.float32),
            pattern,
            pattern,
            pattern,
            pltpu.SemaphoreType.DMA((2, PIECES)),
            pltpu.SemaphoreType.DMA((3,)),
            pltpu.SemaphoreType.DMA((n_sends,)),
            pltpu.SemaphoreType.DMA((n_parts,)),
            pltpu.SemaphoreType.DMA((n_sends,)),
            pltpu.SemaphoreType.DMA((n_parts,)),
            pltpu.SemaphoreType.DMA((n_sends,)),
            pltpu.SemaphoreType.DMA((n_parts,)),
        ],
        compiler_params=pltpu.CompilerParams(
            collective_id=0,
            has_side_effects=True,
            vmem_limit_bytes=40 * 1024 * 1024,
        ),
    )(*[pltpu.with_memory_space_constraint(v, pltpu.HBM) for v in (left_blocks, right_blocks, a_pattern.T, b_pattern.T, keep_mask.T)])


def solution(mesh):
    placed = (P("row", "col"),) * 5
    return jax.shard_map(
        on_device, mesh=mesh, in_specs=placed, out_specs=P("row", "col"), check_vma=False
    )
```
